256 devices in a mesh: sec: 2 (over core), gx: 8 (over z), gy: 16 (over y, x).
Axes of the slice: x: 4, y: 4, z: 8, core: 2. Of those that a mesh axis runs over, the one named last changes fastest.
Arguments:
- air_sea_state: float32 [2, 16, 384, 4096], P('sec', None, 'gx', 'gy'), may hold values from -6 to 6
- diffusion: float32 [2, 16], P('sec'), may hold values from 0.04 to 0.15
- courant: float32 [2, 16], P('sec'), may hold values from 0.1 to 0.35
- exchange_coef: float32 [2, 384, 4096], P('sec', 'gx', 'gy'), may hold values from 0.2 to 1
- src_block: int32 [2, 24576], P('sec', ('gx', 'gy')), may hold values from 0 to 95
- dest_peer: int32 [2, 24576, 1], P('sec', ('gx', 'gy')), may hold values from 0 to 127; in each aligned block of 192 rows (0 to 191, 192 to 383, ..., all dimensions but the last counted through in order) at most 3 rows name the same one
- dest_block: int32 [2, 24576], P('sec', ('gx', 'gy')), may hold values from 0 to 95
- remap_weight: float32 [2, 24576, 128, 128], P('sec', ('gx', 'gy')), may hold values from -0.375 to 0.375
Outputs:
- new_state: float32 [2, 16, 384, 4096], P('sec', None, 'gx', 'gy')
- remapped: float32 [2, 4, 384, 4096], P('sec', None, 'gx', 'gy')
The draws below stay inside these ranges and needn't reach their ends.
Inputs may be any that keep to these rules, and one draw needn't show every extreme that they name: `dest_peer`: among the 192 entries owned by one device (aligned blocks of 192 entries of one component), no destination device is named more than 3 times, and in every draw some device is named exactly 3 times by some owner.
All inputs are finite; a program needn't handle non-finite values.
Results may differ from the reference program's by a relative error of at most 0.0001.
Values sent between devices are 32-bit elements; how exact they have to be, the bound alone decides.
No kernel may reach another device: no remote copies, remote signals or barrier semaphores. Data moves between devices by JAX's collectives and lax.ppermute only.
A program may use at most 64 MiB of HBM per device.

```python
import math
import jax
import jax.numpy as jnp
import numpy as np
from jax import lax

COMPS = 2
LEV = 16
NF = 4
BLK = 128
CX = 48
CY = 256
STEPS_A = 6
STEPS_O = 3
OVL = 2
BPD = 96
EPD = 192
PEERS = 128
CAP = 3
ENTRIES = 24576
NX = 384
NY = 4096
N_GX = 8
N_GY = 16


def set_ends(drawn, stream_key, low, largest):
    extent = drawn.shape
    spot = [jax.random.randint(jax.random.fold_in(stream_key, axis), (), 0, extent[axis]) for axis in range(len(extent))]
    drawn = drawn.at[tuple(spot)].set(low)
    longest = extent.index(max(extent))
    spot[longest] = (spot[longest] + 1) % extent[longest]
    return drawn.at[tuple(spot)].set(largest)


def steps_of(own_key, dims, shards, least, largest):
    factor_of, own = 1.0, jax.random.fold_in(own_key, 6)
    for axis_at, shards_of in shards:
        heights = jnp.exp(jax.random.uniform(jax.random.fold_in(own, axis_at), (shards_of,), jnp.float32, least / len(shards), largest / len(shards)))
        factor_of = factor_of * jnp.repeat(heights, dims[axis_at] // shards_of).reshape([-1 if axis == axis_at else 1 for axis in range(len(dims))])
    return factor_of


def routed_block(rng, own, number, rows, number_of, top, bound, skew):
    sequence = jax.random.permutation(rng, number_of)
    packed, ordinary = shares(number_of, rows * top, bound, skew, True), shares(number_of, rows * top, bound, skew, False)
    places = jnp.arange(number_of)

    def named(sizes, rotation):
        used = int((sizes > 0).sum())
        fixed = max(1, used // 4)
        moved = fixed + (places - fixed + rotation * (used - fixed)) % max(1, number_of - fixed)
        return jnp.zeros((number_of,), jnp.int32).at[sequence[jnp.where(places < fixed, places, moved)]].set(jnp.asarray(sizes, jnp.int32))

    sizes = jnp.where(number % 4 == 0, named(packed, number // 4), named(ordinary, number - number // 4 - 1))
    mixed = jax.random.permutation(jax.random.fold_in(own, 3), number_of)
    source_of, sink = mixed[0:number_of // 2 * 2:2], mixed[1:number_of // 2 * 2:2]
    margin = jnp.minimum(sizes[source_of] - 1, bound - sizes[sink]) // 2
    margin = jnp.where((source_of == sequence[0]) | (sink == sequence[0]) | (sizes[sink] == 0), 0, jnp.maximum(margin, 0))
    moved = jax.random.randint(jax.random.fold_in(own, 4), (number_of // 2,), 0, 1 << 20) % (margin + 1)
    sizes = sizes.at[source_of].add(-moved).at[sink].add(moved)
    labels = jnp.searchsorted(jnp.cumsum(sizes), jnp.arange(rows * top), side="right").astype(jnp.int32)
    grid = labels.reshape(top, rows).T
    grid = grid[jax.random.permutation(jax.random.fold_in(own, 1), rows)]
    rotation = jax.random.randint(jax.random.fold_in(own, 2), (rows, 1), 0, top)
    return jnp.take_along_axis(grid, (jnp.arange(top)[None, :] + rotation) % top, axis=1)


def shares(count, total, most, skew, full):
    loads = [(1 << 20) // math.isqrt(standing ** skew) + 1 for standing in range(1, count + 1)]
    largest = most if full else min(most, max(-(-total // count), total * loads[0] // sum(loads)))
    least = 1 if total - largest >= count - 1 else 0
    counts, surplus = [largest] + [least] * (count - 1), total - largest - least * (count - 1)
    while surplus > 0:
        free = [i for i in range(1, count) if counts[i] < largest] or [i for i in range(1, count) if counts[i] < most]
        whole, left = sum([loads[i] for i in free]), surplus
        for i in free:
            extra = min(most - counts[i], max(1, left * loads[i] // whole), surplus)
            counts[i] = counts[i] + extra
            surplus = surplus - extra
    return np.array(counts)


def scatter_about(key, extent, deviation, most, pieces=(), kind=jnp.bfloat16):
    drawn = deviation * jax.random.normal(key, extent, jnp.float32)
    if pieces:
        drawn = drawn * steps_of(key, extent, pieces, -0.22, 0.18)
    return jnp.clip(drawn, -most, most).astype(kind)


def setup_inputs(seed: int = 0) -> dict:
    arg_keys = jax.random.split(jax.random.key(seed), 9)
    air_sea_state = scatter_about(arg_keys[0], (COMPS, LEV, NX, NY), 1.0, 6.0, ((0, 2), (2, 8), (3, 16)), jnp.float32)
    diffusion = jnp.clip(jnp.exp(math.log(0.15) - 1.3217559 * jax.random.uniform(arg_keys[1], (COMPS, LEV), jnp.float32) ** steps_of(arg_keys[1], (COMPS, LEV), ((0, 2),), -0.2, 0.2)), 0.04, 0.15)
    courant = jnp.clip(0.1 + 0.25 * jax.random.uniform(arg_keys[2], (COMPS, LEV), jnp.float32) ** steps_of(arg_keys[2], (COMPS, LEV), ((0, 2),), -0.2, 0.2), 0.1, 0.35)
    exchange_coef = jnp.clip(jnp.exp(math.log(1.0) - 1.609438 * jax.random.uniform(arg_keys[3], (COMPS, NX, NY), jnp.float32) ** steps_of(arg_keys[3], (COMPS, NX, NY), ((0, 2), (1, 8), (2, 16)), -0.2, 0.2)), 0.2, 1.0)
    src_block = set_ends(jax.random.randint(arg_keys[4], (COMPS, ENTRIES), 0, BPD), jax.random.fold_in(arg_keys[4], 1), 0, BPD - 1).astype(jnp.int32)
    dest_peer_keys = jax.random.split(jax.random.fold_in(arg_keys[5], 1), COMPS * ENTRIES // EPD)
    dest_peer_turns = jax.random.permutation(jax.random.fold_in(arg_keys[5], 3), COMPS * ENTRIES // EPD)
    dest_peer = jax.vmap(lambda own, number: routed_block(jax.random.fold_in(arg_keys[5], 2), own, number, EPD, PEERS, 1, CAP, 2))(dest_peer_keys, dest_peer_turns).reshape((COMPS, ENTRIES, 1))
    dest_block = set_ends(jax.random.randint(arg_keys[6], (COMPS, ENTRIES), 0, BPD), jax.random.fold_in(arg_keys[6], 1), 0, BPD - 1).astype(jnp.int32)
    remap_weight = scatter_about(arg_keys[7], (COMPS, ENTRIES, BLK, BLK), (BLK * OVL) ** -0.5, 0.375, ((0, 2), (1, 128)), jnp.float32)
    return dict(air_sea_state=air_sea_state, diffusion=diffusion, courant=courant, exchange_coef=exchange_coef, src_block=src_block, dest_peer=dest_peer, dest_block=dest_block, remap_weight=remap_weight)


def advance(levels, diffusion, courant):
    padded = jnp.pad(levels, ((0, 0), (0, 0), (1, 1), (1, 1)))
    prev_x = padded[:, :, :-2, 1:-1]
    beside_all = padded[:, :, 2:, 1:-1] + prev_x + padded[:, :, 1:-1, 2:] + padded[:, :, 1:-1, :-2]
    diffuse = diffusion[:, :, None, None]
    carry_rate = courant[:, :, None, None]
    return levels + diffuse * (beside_all - 4.0 * levels) - carry_rate * (levels - prev_x)


def to_blocks(surface):
    shaped = surface.reshape(NF, N_GX, CX, N_GY, CY // BLK, BLK)
    shaped = shaped.transpose(1, 3, 2, 4, 0, 5)
    return shaped.reshape(N_GX * N_GY * BPD, NF, BLK)


def from_blocks(totals):
    shaped = totals.reshape(N_GX, N_GY, CX, CY // BLK, NF, BLK)
    shaped = shaped.transpose(4, 0, 2, 1, 3, 5)
    return shaped.reshape(NF, CX * N_GX, CY * N_GY)


def reference(air_sea_state, diffusion, courant, exchange_coef, src_block, dest_peer, dest_block, remap_weight):
    stepped = air_sea_state
    for sweep_index in range(STEPS_A):
        candidate = advance(stepped, diffusion, courant)
        active = jnp.array([True, sweep_index < STEPS_O])[:, None, None, None]
        stepped = jnp.where(active, candidate, stepped)
    peer_count = N_GX * N_GY
    offsets = (jnp.arange(peer_count, dtype=jnp.int32) * BPD)[:, None]
    totals = [None, None]
    for comp in range(2):
        blocks = to_blocks(stepped[comp, :NF])
        tiles = remap_weight[comp].reshape(peer_count, EPD, BLK, BLK)
        source_rows = src_block[comp].reshape(peer_count, EPD).astype(jnp.int32) + offsets

        def owner_products(pair):
            tile_set, rows_now = pair
            picked = blocks[rows_now]
            return jnp.einsum("eij,efj->efi", tile_set, picked, precision=lax.Precision.HIGHEST)

        products = lax.map(owner_products, (tiles, source_rows)).reshape(peer_count * EPD, NF, BLK)
        target_rows = dest_peer[comp][:, 0].astype(jnp.int32) * BPD + dest_block[comp].astype(jnp.int32)
        totals[1 - comp] = jnp.zeros((peer_count * BPD, NF, BLK), jnp.float32).at[target_rows].add(products)
    remapped = jnp.stack([from_blocks(totals[0]), from_blocks(totals[1])])
    surface = stepped[:, :NF]
    coupling = exchange_coef[:, None]
    new_surface = surface + coupling * jnp.tanh(remapped - surface)
    new_state = jnp.concatenate([new_surface, stepped[:, NF:]], axis=1)
    return new_state, remapped
```

```python
import jax
import jax.numpy as jnp
from jax import lax
from jax.experimental import pallas as pl
from jax.experimental.pallas import tpu as pltpu
from jax.sharding import PartitionSpec as P

LEV = 16
NF = 4
BLK = 128
CX = 48
CY = 256
BPD = 96
EPD = 192
CAP = 3
STEPS_A = 6
STEPS_O = 3
HALO = 8
ROWS = CX + 2 * HALO
COLS = CY + BLK
CHUNK = 16
N_CHUNKS = EPD // CHUNK


def ring(axis, shift):
    count = lax.axis_size(axis)
    return [(i, (i + shift) % count) for i in range(count)]


def inside(meta_ref):
    row = lax.broadcasted_iota(jnp.int32, (ROWS, COLS), 0)
    col = lax.broadcasted_iota(jnp.int32, (ROWS, COLS), 1)
    row = jnp.where(row >= CX + HALO, row - ROWS, row) + meta_ref[0]
    col = jnp.where(col >= CY + BLK // 2, col - COLS, col) + meta_ref[1]
    return (row >= 0) & (row < meta_ref[2]) & (col >= 0) & (col < meta_ref[3])


def extended(tile, top, bottom, from_left, from_right, level):
    lane = lax.broadcasted_iota(jnp.int32, (ROWS, BLK), 1)
    after = pltpu.roll(from_right, (BLK - HALO * level) % BLK, 1)
    before = pltpu.roll(from_left, (2 * BLK - HALO - HALO * level) % BLK, 1)
    beyond = jnp.where(lane < HALO, after, jnp.where(lane >= BLK - HALO, before, 0.0))
    own = jnp.concatenate([tile, bottom, top], axis=0)
    return jnp.concatenate([own, beyond], axis=1)


def evolve(field, keep, diffuse, carry_rate, steps):
    field = field * keep
    centre = 1.0 - 4.0 * diffuse - carry_rate
    upwind = diffuse + carry_rate

    def step(_, u):
        beside = pltpu.roll(u, ROWS - 1, 0) + pltpu.roll(u, 1, 1) + pltpu.roll(u, COLS - 1, 1)
        return (centre * u + upwind * pltpu.roll(u, 1, 0) + diffuse * beside) * keep

    return lax.fori_loop(0, steps, step, field)


def pack_kernel(x_ref, top_ref, bottom_ref, left_ref, right_ref):
    lane = lax.broadcasted_iota(jnp.int32, (ROWS, BLK), 1) // HALO
    left = jnp.zeros((ROWS, BLK), jnp.float32)
    right = jnp.zeros((ROWS, BLK), jnp.float32)
    for level in range(LEV):
        own = jnp.concatenate([x_ref[level], bottom_ref[level], top_ref[level]], axis=0)
        left = jnp.where(lane == level, pltpu.roll(own[:, :BLK], HALO * level, 1), left)
        right = jnp.where(
            lane == level, pltpu.roll(own[:, CY - BLK :], (HALO * level + HALO) % BLK, 1), right
        )
    left_ref[...] = left
    right_ref[...] = right


def surface_kernel(
    meta_ref, rates_ref, route_ref, x_ref, top_ref, bottom_ref, left_ref, right_ref, w_ref,
    slots_ref, surface_ref, w_buf, blocks, keep_ref, sems,
):
    def fetch(part):
        rows = pl.ds(part * CHUNK, CHUNK)
        return pltpu.make_async_copy(w_ref.at[rows], w_buf.at[rows], sems.at[part])

    for part in range(N_CHUNKS):
        fetch(part).start()
    slots_ref[...] = jnp.zeros(slots_ref.shape, jnp.float32)
    keep_ref[...] = inside(meta_ref).astype(jnp.float32)
    for level in range(NF):
        field = extended(
            x_ref[level], top_ref[level], bottom_ref[level], left_ref[...], right_ref[...], level
        )
        field = evolve(field, keep_ref[...], rates_ref[0, level], rates_ref[1, level], meta_ref[4])
        field = field[:CX, :CY]
        surface_ref[level] = field
        high = field.astype(jnp.bfloat16).astype(jnp.float32)
        low = field - high
        for half in range(2):
            cols = slice(half * BLK, (half + 1) * BLK)
            blocks[pl.ds(half * 8 + level, CX, stride=16), :] = high[:, cols]
            blocks[pl.ds(half * 8 + NF + level, CX, stride=16), :] = low[:, cols]

    def entry(e):
        picked = blocks[pl.ds(pl.multiple_of(route_ref[0, e] * 8, 8), 8), :].astype(jnp.bfloat16)
        weight = w_buf[e]
        high = weight.astype(jnp.bfloat16)
        low = (weight - high.astype(jnp.float32)).astype(jnp.bfloat16)
        dims = (((1,), (1,)), ((), ()))
        both = lax.dot_general(picked, high, dims, preferred_element_type=jnp.float32)
        both += lax.dot_general(picked, low, dims, preferred_element_type=jnp.float32)
        slots_ref[route_ref[1, e]] = both[:NF] + both[NF:]

    @pl.loop(0, N_CHUNKS)
    def _(part):
        fetch(part).wait()
        for k in range(CHUNK):
            entry(part * CHUNK + k)


def aloft_kernel(
    meta_ref, rates_ref, x_ref, top_ref, bottom_ref, left_ref, right_ref, out_ref, keep_ref
):
    group = pl.program_id(0) + 1

    @pl.when(group == 1)
    def _():
        keep_ref[...] = inside(meta_ref).astype(jnp.float32)

    for k in range(NF):
        level = group * NF + k
        field = extended(
            x_ref[k], top_ref[k], bottom_ref[k], left_ref[...], right_ref[...], level
        )
        field = evolve(field, keep_ref[...], rates_ref[0, level], rates_ref[1, level], meta_ref[4])
        out_ref[k] = field[:CX, :CY]


def finish_kernel(slots_ref, labels_ref, surface_ref, coef_ref, aloft_ref, state_ref, remapped_ref):
    del aloft_ref
    row = lax.broadcasted_iota(jnp.int32, (BPD, labels_ref.shape[1]), 0)
    block = jnp.where(row < CX, 2 * row, 2 * (row - CX) + 1)
    chosen = (block == labels_ref[...]).astype(jnp.bfloat16)
    dims = (((1,), (0,)), ((), ()))
    for level in range(NF):
        data = slots_ref[pl.ds(level, labels_ref.shape[1], stride=NF), :]
        high = data.astype(jnp.bfloat16)
        low = (data - high.astype(jnp.float32)).astype(jnp.bfloat16)
        total = lax.dot_general(chosen, high, dims, preferred_element_type=jnp.float32)
        total += lax.dot_general(chosen, low, dims, preferred_element_type=jnp.float32)
        total = jnp.concatenate([total[:CX], total[CX:]], axis=1)
        remapped_ref[level] = total
        surface = surface_ref[level]
        state_ref[level] = surface + coef_ref[...] * jnp.tanh(total - surface)


def body(
    air_sea_state, diffusion, courant, exchange_coef, src_block, dest_peer, dest_block, remap_weight
):
    peers = lax.axis_size("gx") * lax.axis_size("gy")
    slots = peers * CAP
    at_x, at_y = lax.axis_index("gx"), lax.axis_index("gy")
    x = air_sea_state[0]
    smem = pl.BlockSpec(memory_space=pltpu.SMEM)
    vmem = pl.BlockSpec(memory_space=pltpu.VMEM)
    limit = pltpu.CompilerParams(vmem_limit_bytes=48 << 20)

    meta = jnp.stack(
        [
            at_x * CX,
            at_y * CY,
            lax.axis_size("gx") * CX,
            lax.axis_size("gy") * CY,
            jnp.where(lax.axis_index("sec") == 0, STEPS_A, STEPS_O),
        ]
    ).astype(jnp.int32)
    rates = jnp.concatenate([diffusion, courant], axis=0)

    with jax.named_scope("routes"):
        target = dest_peer[0][:, 0]
        entry = jnp.arange(EPD, dtype=jnp.int32)
        earlier = (target[:, None] == target[None, :]) & (entry[None, :] < entry[:, None])
        position = target * CAP + jnp.sum(earlier.astype(jnp.int32), axis=1)
        route = jnp.stack([src_block[0], position])
        filled = position[None, :] == jnp.arange(slots, dtype=jnp.int32)[:, None]
        labels = jnp.sum(jnp.where(filled, dest_block[0][None, :] + 1, 0), axis=1) - 1
        labels = lax.all_gather(labels, ("gx", "gy"), axis=0, tiled=False)
        labels = lax.dynamic_slice_in_dim(labels, (at_x * lax.axis_size("gy") + at_y) * CAP, CAP, 1)
        labels = lax.ppermute(labels.reshape(1, slots), "sec", ring("sec", 1))

    with jax.named_scope("halo"):
        top = lax.ppermute(x[:, CX - HALO :], "gx", ring("gx", 1))
        bottom = lax.ppermute(x[:, :HALO], "gx", ring("gx", -1))
        side = jax.ShapeDtypeStruct((ROWS, BLK), jnp.float32)
        left, right = pl.pallas_call(pack_kernel, out_shape=(side, side), name="pack")(
            x, top, bottom
        )
        from_right = lax.ppermute(left, "gy", ring("gy", -1))
        from_left = lax.ppermute(right, "gy", ring("gy", 1))

    tile = pl.BlockSpec((NF, CX, CY), lambda i: (0, 0, 0))
    edge = pl.BlockSpec((NF, HALO, CY), lambda i: (0, 0, 0))
    whole = pl.BlockSpec((ROWS, BLK), lambda i: (0, 0))
    outgoing, surface = pl.pallas_call(
        surface_kernel,
        grid=(1,),
        in_specs=[smem, smem, smem, tile, edge, edge, whole, whole, pl.BlockSpec(memory_space=pl.ANY)],
        out_specs=[pl.BlockSpec((slots, NF, BLK), lambda i: (0, 0, 0)), tile],
        out_shape=(
            jax.ShapeDtypeStruct((slots, NF, BLK), jnp.float32),
            jax.ShapeDtypeStruct((NF, CX, CY), jnp.float32),
        ),
        scratch_shapes=[
            pltpu.VMEM((EPD, BLK, BLK), jnp.float32),
            pltpu.VMEM((BPD * 8, BLK), jnp.float32),
            pltpu.VMEM((ROWS, COLS), jnp.float32),
            pltpu.SemaphoreType.DMA((N_CHUNKS,)),
        ],
        compiler_params=limit,
        name="surface",
    )(meta, rates, route, x, top, bottom, from_left, from_right, remap_weight[0])

    tile_up = pl.BlockSpec((NF, CX, CY), lambda i: (i + 1, 0, 0))
    edge_up = pl.BlockSpec((NF, HALO, CY), lambda i: (i + 1, 0, 0))
    aloft = pl.pallas_call(
        aloft_kernel,
        grid=(LEV // NF - 1,),
        in_specs=[smem, smem, tile_up, edge_up, edge_up, whole, whole],
        out_specs=tile_up,
        out_shape=jax.ShapeDtypeStruct((LEV, CX, CY), jnp.float32),
        scratch_shapes=[pltpu.VMEM((ROWS, COLS), jnp.float32)],
        compiler_params=limit,
        name="aloft",
    )(meta, rates, x, top, bottom, from_left, from_right)

    incoming = lax.all_to_all(
        outgoing.reshape(peers, CAP, NF, BLK), ("gx", "gy"), split_axis=0, concat_axis=0, tiled=True
    )
    incoming = lax.ppermute(incoming, "sec", ring("sec", 1))

    new_state, remapped = pl.pallas_call(
        finish_kernel,
        grid=(1,),
        in_specs=[
            pl.BlockSpec((slots * NF, BLK), lambda i: (0, 0)),
            pl.BlockSpec((1, slots), lambda i: (0, 0)),
            tile,
            pl.BlockSpec((CX, CY), lambda i: (0, 0)),
            pl.BlockSpec(memory_space=pl.ANY),
        ],
        out_specs=[tile, tile],
        out_shape=(
            jax.ShapeDtypeStruct((LEV, CX, CY), jnp.float32),
            jax.ShapeDtypeStruct((NF, CX, CY), jnp.float32),
        ),
        input_output_aliases={4: 0},
        compiler_params=limit,
        name="finish",
    )(incoming.reshape(slots * NF, BLK), labels, surface, exchange_coef[0], aloft)
    return (new_state[None], remapped[None])


def solution(mesh):
    in_specs = (
        P("sec", None, "gx", "gy"),
        P("sec", None),
        P("sec", None),
        P("sec", "gx", "gy"),
        P("sec", ("gx", "gy")),
        P("sec", ("gx", "gy"), None),
        P("sec", ("gx", "gy")),
        P("sec", ("gx", "gy"), None, None),
    )
    out_specs = (P("sec", None, "gx", "gy"), P("sec", None, "gx", "gy"))
    return jax.shard_map(body, mesh=mesh, in_specs=in_specs, out_specs=out_specs, check_vma=False)
```

```python
import jax
import jax.numpy as jnp
from jax import lax
from jax.experimental import pallas as pl
from jax.experimental.pallas import tpu as pltpu
from jax.sharding import PartitionSpec as P

LEV = 16
NF = 4
BLK = 128
CX = 48
CY = 256
BPD = 96
EPD = 192
CAP = 3
STEPS_A = 6
STEPS_O = 3
HALO = 8
ROWS = CX + 2 * HALO
COLS = CY + BLK
CHUNK = 16
N_CHUNKS = EPD // CHUNK
ROWS_PER_PEER = CAP * NF + 1


def ring(axis, shift):
    count = lax.axis_size(axis)
    return [(i, (i + shift) % count) for i in range(count)]


def inside(meta_ref):
    row = lax.broadcasted_iota(jnp.int32, (ROWS, COLS), 0)
    col = lax.broadcasted_iota(jnp.int32, (ROWS, COLS), 1)
    row = jnp.where(row >= CX + HALO, row - ROWS, row) + meta_ref[0]
    col = jnp.where(col >= CY + BLK // 2, col - COLS, col) + meta_ref[1]
    return (row >= 0) & (row < meta_ref[2]) & (col >= 0) & (col < meta_ref[3])


def extended(tile, top, bottom, from_left, from_right, level):
    lane = lax.broadcasted_iota(jnp.int32, (ROWS, BLK), 1)
    after = pltpu.roll(from_right, (BLK - HALO * level) % BLK, 1)
    before = pltpu.roll(from_left, (2 * BLK - HALO - HALO * level) % BLK, 1)
    beyond = jnp.where(lane < HALO, after, jnp.where(lane >= BLK - HALO, before, 0.0))
    own = jnp.concatenate([tile, bottom, top], axis=0)
    return jnp.concatenate([own, beyond], axis=1)


def evolve(field, keep, diffuse, carry_rate, steps):
    field = field * keep
    centre = 1.0 - 4.0 * diffuse - carry_rate
    upwind = diffuse + carry_rate

    def step(_, u):
        beside = pltpu.roll(u, ROWS - 1, 0) + pltpu.roll(u, 1, 1) + pltpu.roll(u, COLS - 1, 1)
        return (centre * u + upwind * pltpu.roll(u, 1, 0) + diffuse * beside) * keep

    return lax.fori_loop(0, steps, step, field)


def pack_kernel(x_ref, top_ref, bottom_ref, left_ref, right_ref):
    lane = lax.broadcasted_iota(jnp.int32, (ROWS, BLK), 1) // HALO
    left = jnp.zeros((ROWS, BLK), jnp.float32)
    right = jnp.zeros((ROWS, BLK), jnp.float32)
    for level in range(LEV):
        own = jnp.concatenate([x_ref[level], bottom_ref[level], top_ref[level]], axis=0)
        left = jnp.where(lane == level, pltpu.roll(own[:, :BLK], HALO * level, 1), left)
        right = jnp.where(
            lane == level, pltpu.roll(own[:, CY - BLK :], (HALO * level + HALO) % BLK, 1), right
        )
    left_ref[...] = left
    right_ref[...] = right


def split_kernel(w_ref, *refs):
    high_ref, low_ref = refs[-2:]
    rows = pl.ds(pl.program_id(0) * CHUNK, CHUNK)
    weight = w_ref[...]
    high = weight.astype(jnp.bfloat16)
    high_ref[rows] = high
    low_ref[rows] = (weight - high.astype(jnp.float32)).astype(jnp.bfloat16)


def surface_kernel(
    meta_ref, rates_ref, route_ref, x_ref, top_ref, bottom_ref, left_ref, right_ref, label_ref,
    high_ref, low_ref, slots_ref, surface_ref, blocks, keep_ref,
):
    slots_ref[...] = jnp.zeros(slots_ref.shape, jnp.float32)
    slots_ref[pl.ds(ROWS_PER_PEER - 1, label_ref.shape[0], stride=ROWS_PER_PEER), :] = label_ref[...]
    keep_ref[...] = inside(meta_ref).astype(jnp.float32)
    for level in range(NF):
        field = extended(
            x_ref[level], top_ref[level], bottom_ref[level], left_ref[...], right_ref[...], level
        )
        field = evolve(field, keep_ref[...], rates_ref[0, level], rates_ref[1, level], meta_ref[4])
        field = field[:CX, :CY]
        surface_ref[level] = field
        high = field.astype(jnp.bfloat16).astype(jnp.float32)
        low = field - high
        for half in range(2):
            cols = slice(half * BLK, (half + 1) * BLK)
            blocks[pl.ds(half * 8 + level, CX, stride=16), :] = high[:, cols]
            blocks[pl.ds(half * 8 + NF + level, CX, stride=16), :] = low[:, cols]

    def entry(e):
        picked = blocks[pl.ds(pl.multiple_of(route_ref[0, e] * 8, 8), 8), :].astype(jnp.bfloat16)
        dims = (((1,), (1,)), ((), ()))
        both = lax.dot_general(picked, high_ref[e], dims, preferred_element_type=jnp.float32)
        both += lax.dot_general(picked, low_ref[e], dims, preferred_element_type=jnp.float32)
        slots_ref[pl.ds(route_ref[1, e], NF), :] = both[:NF] + both[NF:]

    @pl.loop(0, N_CHUNKS)
    def _(part):
        for k in range(CHUNK):
            entry(part * CHUNK + k)


def aloft_kernel(
    meta_ref, rates_ref, x_ref, top_ref, bottom_ref, left_ref, right_ref, out_ref, keep_ref
):
    group = pl.program_id(0) + 1

    @pl.when(group == 1)
    def _():
        keep_ref[...] = inside(meta_ref).astype(jnp.float32)

    for k in range(NF):
        level = group * NF + k
        field = extended(
            x_ref[k], top_ref[k], bottom_ref[k], left_ref[...], right_ref[...], level
        )
        field = evolve(field, keep_ref[...], rates_ref[0, level], rates_ref[1, level], meta_ref[4])
        out_ref[k] = field[:CX, :CY]


def finish_kernel(slots_ref, surface_ref, coef_ref, aloft_ref, state_ref, remapped_ref):
    del aloft_ref
    peers = slots_ref.shape[0] // ROWS_PER_PEER
    labels = slots_ref[pl.ds(ROWS_PER_PEER - 1, peers, stride=ROWS_PER_PEER), :].T
    row = lax.broadcasted_iota(jnp.int32, (BPD, peers), 0)
    block = jnp.where(row < CX, 2 * row, 2 * (row - CX) + 1).astype(jnp.float32)
    chosen = [(block == labels[k : k + 1]).astype(jnp.bfloat16) for k in range(CAP)]
    dims = (((1,), (0,)), ((), ()))
    for level in range(NF):
        total = jnp.zeros((BPD, BLK), jnp.float32)
        for k in range(CAP):
            data = slots_ref[pl.ds(k * NF + level, peers, stride=ROWS_PER_PEER), :]
            high = data.astype(jnp.bfloat16)
            low = (data - high.astype(jnp.float32)).astype(jnp.bfloat16)
            total += lax.dot_general(chosen[k], high, dims, preferred_element_type=jnp.float32)
            total += lax.dot_general(chosen[k], low, dims, preferred_element_type=jnp.float32)
        total = jnp.concatenate([total[:CX], total[CX:]], axis=1)
        remapped_ref[level] = total
        surface = surface_ref[level]
        state_ref[level] = surface + coef_ref[...] * jnp.tanh(total - surface)


def body(
    air_sea_state, diffusion, courant, exchange_coef, src_block, dest_peer, dest_block, remap_weight
):
    peers = lax.axis_size("gx") * lax.axis_size("gy")
    rows_out = peers * ROWS_PER_PEER
    at_x, at_y = lax.axis_index("gx"), lax.axis_index("gy")
    x = air_sea_state[0]
    smem = pl.BlockSpec(memory_space=pltpu.SMEM)
    vmem = pl.BlockSpec(memory_space=pltpu.VMEM)

    def limit(mib):
        return pltpu.CompilerParams(vmem_limit_bytes=mib << 20)

    meta = jnp.stack(
        [
            at_x * CX,
            at_y * CY,
            lax.axis_size("gx") * CX,
            lax.axis_size("gy") * CY,
            jnp.where(lax.axis_index("sec") == 0, STEPS_A, STEPS_O),
        ]
    ).astype(jnp.int32)
    rates = jnp.concatenate([diffusion, courant], axis=0)

    with jax.named_scope("routes"):
        target = dest_peer[0][:, 0]
        entry = jnp.arange(EPD, dtype=jnp.int32)
        earlier = (target[:, None] == target[None, :]) & (entry[None, :] < entry[:, None])
        rank = jnp.sum(earlier.astype(jnp.int32), axis=1)
        route = jnp.stack([src_block[0], target * ROWS_PER_PEER + rank * NF])
        to_peer = target[None, :] == jnp.arange(peers, dtype=jnp.int32)[:, None]
        label = [
            jnp.sum(jnp.where(to_peer & (rank == k)[None, :], dest_block[0][None, :] + 1, 0), axis=1)
            for k in range(CAP)
        ]
        label = jnp.stack(label, axis=1).astype(jnp.float32) - 1.0
        label = jnp.pad(label, ((0, 0), (0, BLK - CAP)), constant_values=-1.0)

    with jax.named_scope("split"):
        part = pl.BlockSpec((CHUNK, BLK, BLK), lambda i: (i, 0, 0))
        half = pltpu.VMEM((EPD, BLK, BLK), jnp.bfloat16)
        high, low = pl.pallas_call(
            split_kernel,
            grid=(N_CHUNKS,),
            in_specs=[part] + [pl.BlockSpec(memory_space=pl.ANY)] * 4,
            out_specs=[vmem, vmem],
            out_shape=(half, half),
            compiler_params=limit(6),
            name="split",
        )(
            pltpu.with_memory_space_constraint(remap_weight[0], pltpu.HBM), meta, rates, route, label
        )

    with jax.named_scope("halo"):
        top = lax.ppermute(x[:, CX - HALO :], "gx", ring("gx", 1))
        bottom = lax.ppermute(x[:, :HALO], "gx", ring("gx", -1))
        side = jax.ShapeDtypeStruct((ROWS, BLK), jnp.float32)
        left, right = pl.pallas_call(
            pack_kernel, out_shape=(side, side), compiler_params=limit(3), name="pack"
        )(x, top, bottom)
        from_right = lax.ppermute(left, "gy", ring("gy", -1))
        from_left = lax.ppermute(right, "gy", ring("gy", 1))

    tile = pl.BlockSpec((NF, CX, CY), lambda i: (0, 0, 0))
    edge = pl.BlockSpec((NF, HALO, CY), lambda i: (0, 0, 0))
    whole = pl.BlockSpec((ROWS, BLK), lambda i: (0, 0))
    outgoing, surface = pl.pallas_call(
        surface_kernel,
        grid=(1,),
        in_specs=[
            smem, smem, smem, tile, edge, edge, whole, whole,
            pl.BlockSpec((peers, BLK), lambda i: (0, 0)), vmem, vmem,
        ],
        out_specs=[pl.BlockSpec((rows_out, BLK), lambda i: (0, 0)), tile],
        out_shape=(
            jax.ShapeDtypeStruct((rows_out, BLK), jnp.float32),
            jax.ShapeDtypeStruct((NF, CX, CY), jnp.float32),
        ),
        scratch_shapes=[
            pltpu.VMEM((BPD * 8, BLK), jnp.float32),
            pltpu.VMEM((ROWS, COLS), jnp.float32),
        ],
        compiler_params=limit(6),
        name="surface",
    )(meta, rates, route, x, top, bottom, from_left, from_right, label, high, low)

    tile_up = pl.BlockSpec((NF, CX, CY), lambda i: (i + 1, 0, 0))
    edge_up = pl.BlockSpec((NF, HALO, CY), lambda i: (i + 1, 0, 0))
    aloft = pl.pallas_call(
        aloft_kernel,
        grid=(LEV // NF - 1,),
        in_specs=[smem, smem, tile_up, edge_up, edge_up, whole, whole],
        out_specs=tile_up,
        out_shape=jax.ShapeDtypeStruct((LEV, CX, CY), jnp.float32),
        scratch_shapes=[pltpu.VMEM((ROWS, COLS), jnp.float32)],
        compiler_params=limit(4),
        name="aloft",
    )(meta, rates, x, top, bottom, from_left, from_right)

    incoming = lax.all_to_all(
        outgoing.reshape(peers, ROWS_PER_PEER, 1, BLK), ("gx", "gy"), split_axis=0, concat_axis=0, tiled=True
    )
    incoming = lax.ppermute(incoming.reshape(rows_out, BLK), "sec", ring("sec", 1))

    new_state, remapped = pl.pallas_call(
        finish_kernel,
        grid=(1,),
        in_specs=[
            pl.BlockSpec((rows_out, BLK), lambda i: (0, 0)),
            tile,
            pl.BlockSpec((CX, CY), lambda i: (0, 0)),
            pl.BlockSpec(memory_space=pl.ANY),
        ],
        out_specs=[tile, tile],
        out_shape=(
            jax.ShapeDtypeStruct((LEV, CX, CY), jnp.float32),
            jax.ShapeDtypeStruct((NF, CX, CY), jnp.float32),
        ),
        input_output_aliases={3: 0},
        compiler_params=limit(5),
        name="finish",
    )(incoming, surface, exchange_coef[0], aloft)
    return (new_state[None], remapped[None])


def solution(mesh):
    in_specs = (
        P("sec", None, "gx", "gy"),
        P("sec", None),
        P("sec", None),
        P("sec", "gx", "gy"),
        P("sec", ("gx", "gy")),
        P("sec", ("gx", "gy"), None),
        P("sec", ("gx", "gy")),
        P("sec", ("gx", "gy"), None, None),
    )
    out_specs = (P("sec", None, "gx", "gy"), P("sec", None, "gx", "gy"))
    return jax.shard_map(body, mesh=mesh, in_specs=in_specs, out_specs=out_specs, check_vma=False)
```

```python
import jax
import jax.numpy as jnp
from jax import lax
from jax.experimental import pallas as pl
from jax.experimental.pallas import tpu as pltpu
from jax.sharding import PartitionSpec as P

LEV = 16
NF = 4
BLK = 128
CX = 48
CY = 256
BPD = 96
EPD = 192
CAP = 3
STEPS_A = 6
STEPS_O = 3
HALO = 8
ROWS = CX + 2 * HALO
COLS = CY + BLK
CHUNK = 16
N_CHUNKS = EPD // CHUNK
ROWS_PER_PEER = CAP * NF + 1
UNROLL = 8


def ring(axis, shift):
    count = lax.axis_size(axis)
    return [(i, (i + shift) % count) for i in range(count)]


def inside(meta_ref):
    row = lax.broadcasted_iota(jnp.int32, (ROWS, COLS), 0)
    col = lax.broadcasted_iota(jnp.int32, (ROWS, COLS), 1)
    row = jnp.where(row >= CX + HALO, row - ROWS, row) + meta_ref[0]
    col = jnp.where(col >= CY + BLK // 2, col - COLS, col) + meta_ref[1]
    return (row >= 0) & (row < meta_ref[2]) & (col >= 0) & (col < meta_ref[3])


def extended(tile, top, bottom, from_left, from_right, level):
    lane = lax.broadcasted_iota(jnp.int32, (ROWS, BLK), 1)
    after = pltpu.roll(from_right, (BLK - HALO * level) % BLK, 1)
    before = pltpu.roll(from_left, (2 * BLK - HALO - HALO * level) % BLK, 1)
    beyond = jnp.where(lane < HALO, after, jnp.where(lane >= BLK - HALO, before, 0.0))
    own = jnp.concatenate([tile, bottom, top], axis=0)
    return jnp.concatenate([own, beyond], axis=1)


def evolve(field, keep, diffuse, carry_rate, steps):
    field = field * keep
    centre = 1.0 - 4.0 * diffuse - carry_rate
    upwind = diffuse + carry_rate

    def step(_, u):
        beside = pltpu.roll(u, ROWS - 1, 0) + pltpu.roll(u, 1, 1) + pltpu.roll(u, COLS - 1, 1)
        return (centre * u + upwind * pltpu.roll(u, 1, 0) + diffuse * beside) * keep

    return lax.fori_loop(0, steps, step, field)


def prepare_kernel(
    w_ref, x_ref, source_ref, peer_ref, block_ref, meta_ref,
    halves_ref, route_ref, label_ref, left_ref, right_ref, w_buf, x_buf, w_sems, x_sem,
):
    def fetch(part):
        rows = pl.ds(part * CHUNK, CHUNK)
        return pltpu.make_async_copy(w_ref.at[rows], w_buf.at[rows], w_sems.at[part])

    tile = pltpu.make_async_copy(x_ref, x_buf, x_sem)
    for part in range(2):
        fetch(part).start()
    tile.start()
    for part in range(2, N_CHUNKS):
        fetch(part).start()

    target = peer_ref[...]
    same = jnp.broadcast_to(target.astype(jnp.float32), (EPD, EPD))
    same = same == same.T
    first = lax.broadcasted_iota(jnp.int32, (EPD, EPD), 0)
    second = lax.broadcasted_iota(jnp.int32, (EPD, EPD), 1)
    rank = jnp.sum((same & (first < second)).astype(jnp.int32), axis=0, keepdims=True)
    route_ref[0:1] = source_ref[...] * 8
    route_ref[1:2] = target * ROWS_PER_PEER + rank * NF
    peers = label_ref.shape[0]
    to_peer = lax.broadcasted_iota(jnp.int32, (peers, EPD), 0) == target
    lane = lax.broadcasted_iota(jnp.int32, (peers, BLK), 1)
    label = jnp.full((peers, BLK), -1.0, jnp.float32)
    value = block_ref[...].astype(jnp.float32) + 1.0
    for k in range(CAP):
        named = jnp.where(to_peer & (rank == k), value, 0.0)
        label = jnp.where(lane == k, jnp.sum(named, axis=1, keepdims=True) - 1.0, label)
    label_ref[...] = label

    tile.wait()
    lane = lax.broadcasted_iota(jnp.int32, (CX, BLK), 1) // HALO
    left = jnp.zeros((CX, BLK), jnp.float32)
    right = jnp.zeros((CX, BLK), jnp.float32)
    for level in range(LEV):
        left, right = packed(x_buf[level], left, right, lane, level)
    left_ref[...] = left
    right_ref[...] = right

    @pl.loop(0, N_CHUNKS)
    def _(part):
        fetch(part).wait()
        for k in range(CHUNK):
            weight = w_buf[part * CHUNK + k]
            high = weight.astype(jnp.bfloat16)
            low = (weight - high.astype(jnp.float32)).astype(jnp.bfloat16)
            pair = part * (CHUNK // 2) + k // 2
            rows = slice(k % 2 * BLK, (k % 2 + 1) * BLK)
            halves_ref[pair, rows, :BLK] = high
            halves_ref[pair, rows, BLK:] = low


def packed(rows, left, right, lane, level):
    left = jnp.where(lane == level, pltpu.roll(rows[:, :BLK], HALO * level, 1), left)
    shift = (HALO * level + HALO) % BLK
    right = jnp.where(lane == level, pltpu.roll(rows[:, CY - BLK :], shift, 1), right)
    return left, right


def pack_kernel(top_ref, bottom_ref, left_in, right_in, left_ref, right_ref):
    lane = lax.broadcasted_iota(jnp.int32, (2 * HALO, BLK), 1) // HALO
    left = jnp.zeros((2 * HALO, BLK), jnp.float32)
    right = jnp.zeros((2 * HALO, BLK), jnp.float32)
    for level in range(LEV):
        rows = jnp.concatenate([bottom_ref[level], top_ref[level]], axis=0)
        left, right = packed(rows, left, right, lane, level)
    left_ref[:CX] = left_in[...]
    left_ref[CX:] = left
    right_ref[:CX] = right_in[...]
    right_ref[CX:] = right


def surface_kernel(
    meta_ref, diffusion_ref, courant_ref, route_ref, x_ref, top_ref, bottom_ref, left_ref, right_ref, label_ref,
    halves_ref, slots_ref, surface_ref, blocks, keep_ref,
):
    slots_ref[...] = jnp.zeros(slots_ref.shape, jnp.float32)
    slots_ref[pl.ds(ROWS_PER_PEER - 1, label_ref.shape[0], stride=ROWS_PER_PEER), :] = label_ref[...]
    keep_ref[...] = inside(meta_ref).astype(jnp.float32)
    for level in range(NF):
        field = extended(
            x_ref[level], top_ref[level], bottom_ref[level], left_ref[...], right_ref[...], level
        )
        field = evolve(field, keep_ref[...], diffusion_ref[0, level], courant_ref[0, level], meta_ref[4])
        field = field[:CX, :CY]
        surface_ref[level] = field
        high = field.astype(jnp.bfloat16).astype(jnp.float32)
        low = field - high
        for half in range(2):
            cols = slice(half * BLK, (half + 1) * BLK)
            blocks[pl.ds(half * 8 + level, CX, stride=16), :] = high[:, cols]
            blocks[pl.ds(half * 8 + NF + level, CX, stride=16), :] = low[:, cols]

    def pair(p):
        def picked(e):
            return blocks[pl.ds(pl.multiple_of(route_ref[0, e], 8), 8), :]

        rows = jnp.concatenate([picked(2 * p), picked(2 * p + 1)], axis=0).astype(jnp.bfloat16)
        both = lax.dot_general(
            jnp.concatenate([rows, rows], axis=1),
            halves_ref[p],
            (((1,), (1,)), ((), ())),
            preferred_element_type=jnp.float32,
        )
        one = both[0:8, :BLK]
        two = both[8:16, BLK:]
        slots_ref[pl.ds(route_ref[1, 2 * p], NF), :] = one[:NF] + one[NF:]
        slots_ref[pl.ds(route_ref[1, 2 * p + 1], NF), :] = two[:NF] + two[NF:]

    @pl.loop(0, EPD // 2, step=UNROLL)
    def _(start):
        for k in range(UNROLL):
            pair(start + k)


def aloft_kernel(
    meta_ref, diffusion_ref, courant_ref, x_ref, top_ref, bottom_ref, left_ref, right_ref, out_ref, keep_ref
):
    group = pl.program_id(0) + 1

    @pl.when(group == 1)
    def _():
        keep_ref[...] = inside(meta_ref).astype(jnp.float32)

    for k in range(NF):
        level = group * NF + k
        field = extended(
            x_ref[k], top_ref[k], bottom_ref[k], left_ref[...], right_ref[...], level
        )
        field = evolve(field, keep_ref[...], diffusion_ref[0, level], courant_ref[0, level], meta_ref[4])
        out_ref[k] = field[:CX, :CY]


def finish_kernel(slots_ref, surface_ref, coef_ref, aloft_ref, state_ref, remapped_ref):
    del aloft_ref
    peers = slots_ref.shape[0] // ROWS_PER_PEER
    labels = slots_ref[pl.ds(ROWS_PER_PEER - 1, peers, stride=ROWS_PER_PEER), :].T
    row = lax.broadcasted_iota(jnp.int32, (BPD, peers), 0)
    block = jnp.where(row < CX, 2 * row, 2 * (row - CX) + 1).astype(jnp.float32)
    chosen = [(block == labels[k : k + 1]).astype(jnp.bfloat16) for k in range(CAP)]
    dims = (((1,), (0,)), ((), ()))
    for level in range(NF):
        total = jnp.zeros((BPD, BLK), jnp.float32)
        for k in range(CAP):
            data = slots_ref[pl.ds(k * NF + level, peers, stride=ROWS_PER_PEER), :]
            high = data.astype(jnp.bfloat16)
            low = (data - high.astype(jnp.float32)).astype(jnp.bfloat16)
            total += lax.dot_general(chosen[k], high, dims, preferred_element_type=jnp.float32)
            total += lax.dot_general(chosen[k], low, dims, preferred_element_type=jnp.float32)
        total = jnp.concatenate([total[:CX], total[CX:]], axis=1)
        remapped_ref[level] = total
        surface = surface_ref[level]
        state_ref[level] = surface + coef_ref[...] * jnp.tanh(total - surface)


def body(
    air_sea_state, diffusion, courant, exchange_coef, src_block, dest_peer, dest_block, remap_weight
):
    peers = lax.axis_size("gx") * lax.axis_size("gy")
    rows_out = peers * ROWS_PER_PEER
    at_x, at_y = lax.axis_index("gx"), lax.axis_index("gy")
    x = air_sea_state[0]
    smem = pl.BlockSpec(memory_space=pltpu.SMEM)
    vmem = pl.BlockSpec(memory_space=pltpu.VMEM)
    anywhere = pl.BlockSpec(memory_space=pl.ANY)

    def limit(mib):
        return pltpu.CompilerParams(vmem_limit_bytes=mib << 20)

    meta = jnp.stack(
        [
            at_x * CX,
            at_y * CY,
            lax.axis_size("gx") * CX,
            lax.axis_size("gy") * CY,
            jnp.where(lax.axis_index("sec") == 0, STEPS_A, STEPS_O),
        ]
    ).astype(jnp.int32)
    with jax.named_scope("halo"):
        top = lax.ppermute(x[:, CX - HALO :], "gx", ring("gx", 1))
        bottom = lax.ppermute(x[:, :HALO], "gx", ring("gx", -1))

    with jax.named_scope("prepare"):
        centre = jax.ShapeDtypeStruct((CX, BLK), jnp.float32)
        halves, route, label, left, right = pl.pallas_call(
            prepare_kernel,
            in_specs=[anywhere, anywhere, vmem, vmem, vmem, anywhere],
            out_specs=[vmem] * 5,
            out_shape=(
                pltpu.VMEM((EPD // 2, 2 * BLK, 2 * BLK), jnp.bfloat16),
                jax.ShapeDtypeStruct((2, EPD), jnp.int32),
                jax.ShapeDtypeStruct((peers, BLK), jnp.float32),
                centre,
                centre,
            ),
            scratch_shapes=[
                pltpu.VMEM((EPD, BLK, BLK), jnp.float32),
                pltpu.VMEM((LEV, CX, CY), jnp.float32),
                pltpu.SemaphoreType.DMA((N_CHUNKS,)),
                pltpu.SemaphoreType.DMA,
            ],
            compiler_params=limit(18),
            name="prepare",
        )(
            pltpu.with_memory_space_constraint(remap_weight[0], pltpu.HBM),
            pltpu.with_memory_space_constraint(x, pltpu.HBM),
            src_block,
            dest_peer.reshape(1, EPD),
            dest_block,
            meta,
        )

    with jax.named_scope("halo"):
        side = jax.ShapeDtypeStruct((ROWS, BLK), jnp.float32)
        left, right = pl.pallas_call(
            pack_kernel, out_shape=(side, side), compiler_params=limit(2), name="pack"
        )(top, bottom, left, right)
        from_right = lax.ppermute(left, "gy", ring("gy", -1))
        from_left = lax.ppermute(right, "gy", ring("gy", 1))

    tile = pl.BlockSpec((NF, CX, CY), lambda i: (0, 0, 0))
    edge = pl.BlockSpec((NF, HALO, CY), lambda i: (0, 0, 0))
    whole = pl.BlockSpec((ROWS, BLK), lambda i: (0, 0))
    outgoing, surface = pl.pallas_call(
        surface_kernel,
        grid=(1,),
        in_specs=[
            smem, smem, smem, smem, tile, edge, edge, whole, whole,
            pl.BlockSpec((peers, BLK), lambda i: (0, 0)), vmem,
        ],
        out_specs=[pl.BlockSpec((rows_out, BLK), lambda i: (0, 0)), tile],
        out_shape=(
            jax.ShapeDtypeStruct((rows_out, BLK), jnp.float32),
            jax.ShapeDtypeStruct((NF, CX, CY), jnp.float32),
        ),
        scratch_shapes=[
            pltpu.VMEM((BPD * 8, BLK), jnp.float32),
            pltpu.VMEM((ROWS, COLS), jnp.float32),
        ],
        compiler_params=limit(6),
        name="surface",
    )(
        meta, diffusion, courant, route, x, top, bottom, from_left, from_right, label, halves
    )

    tile_up = pl.BlockSpec((NF, CX, CY), lambda i: (i + 1, 0, 0))
    edge_up = pl.BlockSpec((NF, HALO, CY), lambda i: (i + 1, 0, 0))
    aloft = pl.pallas_call(
        aloft_kernel,
        grid=(LEV // NF - 1,),
        in_specs=[smem, smem, smem, tile_up, edge_up, edge_up, whole, whole],
        out_specs=tile_up,
        out_shape=jax.ShapeDtypeStruct((LEV, CX, CY), jnp.float32),
        scratch_shapes=[pltpu.VMEM((ROWS, COLS), jnp.float32)],
        compiler_params=limit(4),
        name="aloft",
    )(meta, diffusion, courant, x, top, bottom, from_left, from_right)

    outgoing = lax.ppermute(outgoing, "sec", ring("sec", 1))
    incoming = lax.all_to_all(
        outgoing.reshape(peers, ROWS_PER_PEER, 1, BLK), ("gx", "gy"), split_axis=0, concat_axis=0, tiled=True
    )
    incoming = incoming.reshape(rows_out, BLK)

    new_state, remapped = pl.pallas_call(
        finish_kernel,
        grid=(1,),
        in_specs=[
            pl.BlockSpec((rows_out, BLK), lambda i: (0, 0)),
            tile,
            pl.BlockSpec((CX, CY), lambda i: (0, 0)),
            pl.BlockSpec(memory_space=pl.ANY),
        ],
        out_specs=[tile, tile],
        out_shape=(
            jax.ShapeDtypeStruct((LEV, CX, CY), jnp.float32),
            jax.ShapeDtypeStruct((NF, CX, CY), jnp.float32),
        ),
        input_output_aliases={3: 0},
        compiler_params=limit(5),
        name="finish",
    )(incoming, surface, exchange_coef[0], aloft)
    return (new_state[None], remapped[None])


def solution(mesh):
    in_specs = (
        P("sec", None, "gx", "gy"),
        P("sec", None),
        P("sec", None),
        P("sec", "gx", "gy"),
        P("sec", ("gx", "gy")),
        P("sec", ("gx", "gy"), None),
        P("sec", ("gx", "gy")),
        P("sec", ("gx", "gy"), None, None),
    )
    out_specs = (P("sec", None, "gx", "gy"), P("sec", None, "gx", "gy"))
    return jax.shard_map(body, mesh=mesh, in_specs=in_specs, out_specs=out_specs, check_vma=False)
```

```python
import jax
import jax.numpy as jnp
from jax import lax
from jax.experimental import pallas as pl
from jax.experimental.pallas import tpu as pltpu
from jax.sharding import PartitionSpec as P

LEV = 16
NF = 4
BLK = 128
CX = 48
CY = 256
BPD = 96
EPD = 192
CAP = 3
STEPS_A = 6
STEPS_O = 3
HALO = 8
ROWS = CX + 2 * HALO
COLS = CY + BLK
CHUNK = 16
N_CHUNKS = EPD // CHUNK
ROWS_PER_PEER = CAP * NF + 1
UNROLL = 36
LATER = 3
DEPTH = 4


def ring(axis, shift):
    count = lax.axis_size(axis)
    return [(i, (i + shift) % count) for i in range(count)]


def inside(meta_ref):
    row = lax.broadcasted_iota(jnp.int32, (ROWS, COLS), 0)
    col = lax.broadcasted_iota(jnp.int32, (ROWS, COLS), 1)
    row = jnp.where(row >= CX + HALO, row - ROWS, row) + meta_ref[0]
    col = jnp.where(col >= CY + BLK // 2, col - COLS, col) + meta_ref[1]
    return (row >= 0) & (row < meta_ref[2]) & (col >= 0) & (col < meta_ref[3])


def extended(tile, top, bottom, from_left, from_right, level):
    lane = lax.broadcasted_iota(jnp.int32, (ROWS, BLK), 1)
    after = pltpu.roll(from_right, (BLK - HALO * level) % BLK, 1)
    before = pltpu.roll(from_left, (2 * BLK - HALO - HALO * level) % BLK, 1)
    beyond = jnp.where(lane < HALO, after, jnp.where(lane >= BLK - HALO, before, 0.0))
    own = jnp.concatenate([tile, bottom, top], axis=0)
    return jnp.concatenate([own, beyond], axis=1)


def evolve(fields, keep_ref, rates, steps):
    def step(u, diffuse, carry_rate):
        beside = pltpu.roll(u, ROWS - 1, 0) + pltpu.roll(u, 1, 1) + pltpu.roll(u, COLS - 1, 1)
        upwind = (diffuse + carry_rate) * pltpu.roll(u, 1, 0)
        centre = (1.0 - 4.0 * diffuse - carry_rate) * u
        return (centre + upwind + diffuse * beside) * keep_ref[...]

    def advance(_, now):
        for _ in range(STEPS_O):
            now = tuple(step(u, *rate) for u, rate in zip(now, rates))
        return now

    fields = tuple(u * keep_ref[...] for u in fields)
    return lax.fori_loop(0, steps // STEPS_O, advance, fields)


def extended_group(meta_ref, rate_refs, x_ref, top_ref, bottom_ref, left_ref, right_ref, keep_ref, first):
    fields, rates = [], []
    for k in range(NF):
        fields.append(
            extended(x_ref[k], top_ref[k], bottom_ref[k], left_ref[...], right_ref[...], first + k)
        )
        rates.append(tuple(ref[0, first + k] for ref in rate_refs))
    fields = evolve(fields, keep_ref, rates, meta_ref[4])
    return [u[:CX, :CY] for u in fields]


def split_parts(w_ref, w_buf, sems, halves_ref, first):
    def fetch(part):
        rows = pl.ds(part * CHUNK, CHUNK)
        whence = w_ref.at[pl.ds((first + part) * CHUNK, CHUNK)]
        return pltpu.make_async_copy(whence, w_buf.at[rows], sems.at[part])

    def begin():
        for part in range(min(DEPTH, sems.shape[0])):
            fetch(part).start()

    def finish():
        @pl.loop(0, sems.shape[0])
        def _(part):
            fetch(part).wait()

            @pl.when(part + DEPTH < sems.shape[0])
            def _():
                fetch(part + DEPTH).start()

            for k in range(CHUNK):
                weight = w_buf[part * CHUNK + k].T
                high = weight.astype(jnp.bfloat16)
                low = (weight - high.astype(jnp.float32)).astype(jnp.bfloat16)
                pair = part * (CHUNK // 2) + k // 2
                cols = slice(k % 2 * BLK, (k % 2 + 1) * BLK)
                halves_ref[pair, :BLK, cols] = high
                halves_ref[pair, BLK:, cols] = low

    return begin, finish


def prepare_kernel(
    w_ref, x_ref, meta_ref, halves_ref, left_ref, right_ref, w_buf, x_buf, w_sems, x_sem
):
    del meta_ref
    tile = pltpu.make_async_copy(x_ref, x_buf, x_sem)
    tile.start()
    begin, finish = split_parts(w_ref, w_buf, w_sems, halves_ref, 0)
    begin()
    tile.wait()
    lane = lax.broadcasted_iota(jnp.int32, (CX, BLK), 1) // HALO
    left = jnp.zeros((CX, BLK), jnp.float32)
    right = jnp.zeros((CX, BLK), jnp.float32)
    for level in range(LEV):
        left, right = packed(x_buf[level], left, right, lane, level)
    left_ref[...] = left
    right_ref[...] = right
    finish()


def route_kernel(
    w_ref, source_ref, peer_ref, block_ref, after_ref, halves_ref, route_ref, label_ref, w_buf, sems
):
    del after_ref
    begin, finish = split_parts(w_ref, w_buf, sems, halves_ref, N_CHUNKS - sems.shape[0])
    begin()
    target = peer_ref[...]
    column = jnp.broadcast_to(target.astype(jnp.float32), (8, EPD)).T[:, :1].astype(jnp.int32)
    first = lax.broadcasted_iota(jnp.int32, (EPD, EPD), 0)
    second = lax.broadcasted_iota(jnp.int32, (EPD, EPD), 1)
    earlier = (column == target) & (first < second)
    rank = jnp.sum(earlier.astype(jnp.int32), axis=0, keepdims=True)
    route_ref[0:1] = source_ref[...] * 8
    route_ref[1:2] = target * ROWS_PER_PEER + rank * NF
    peers = label_ref.shape[0]
    to_peer = lax.broadcasted_iota(jnp.int32, (peers, EPD), 0) == target
    slot = lax.broadcasted_iota(jnp.int32, (BLK, EPD), 0) == rank
    value = jnp.where(slot, block_ref[...].astype(jnp.float32) + 1.0, 0.0)
    label_ref[...] = lax.dot_general(
        to_peer.astype(jnp.bfloat16),
        value.astype(jnp.bfloat16),
        (((1,), (1,)), ((), ())),
        preferred_element_type=jnp.float32,
    ) - 1.0
    finish()


def packed(rows, left, right, lane, level):
    left = jnp.where(lane == level, pltpu.roll(rows[:, :BLK], HALO * level, 1), left)
    shift = (HALO * level + HALO) % BLK
    right = jnp.where(lane == level, pltpu.roll(rows[:, CY - BLK :], shift, 1), right)
    return left, right


def pack_kernel(top_ref, bottom_ref, left_in, right_in, left_ref, right_ref):
    lane = lax.broadcasted_iota(jnp.int32, (2 * HALO, BLK), 1) // HALO
    left = jnp.zeros((2 * HALO, BLK), jnp.float32)
    right = jnp.zeros((2 * HALO, BLK), jnp.float32)
    for level in range(LEV):
        rows = jnp.concatenate([bottom_ref[level], top_ref[level]], axis=0)
        left, right = packed(rows, left, right, lane, level)
    left_ref[:CX] = left_in[...]
    left_ref[CX:] = left
    right_ref[:CX] = right_in[...]
    right_ref[CX:] = right


def surface_kernel(
    meta_ref, diffusion_ref, courant_ref, route_ref, x_ref, top_ref, bottom_ref, left_ref, right_ref, label_ref,
    halves_ref, later_ref, slots_ref, surface_ref, blocks, keep_ref,
):
    slots_ref[...] = jnp.zeros(slots_ref.shape, jnp.float32)
    slots_ref[pl.ds(ROWS_PER_PEER - 1, label_ref.shape[0], stride=ROWS_PER_PEER), :] = label_ref[...]
    keep_ref[...] = inside(meta_ref).astype(jnp.float32)
    fields = extended_group(
        meta_ref, (diffusion_ref, courant_ref), x_ref, top_ref, bottom_ref, left_ref, right_ref,
        keep_ref, 0,
    )
    for level, field in enumerate(fields):
        surface_ref[level] = field
        high = field.astype(jnp.bfloat16).astype(jnp.float32)
        low = field - high
        for half in range(2):
            cols = slice(half * BLK, (half + 1) * BLK)
            blocks[pl.ds(half * 8 + level, CX, stride=16), :] = high[:, cols]
            blocks[pl.ds(half * 8 + NF + level, CX, stride=16), :] = low[:, cols]

    def pair(ref, p, first):
        def picked(e):
            return blocks[pl.ds(pl.multiple_of(route_ref[0, e], 8), 8), :]

        e = 2 * (p + first)
        rows = jnp.concatenate([picked(e), picked(e + 1)], axis=0).astype(jnp.bfloat16)
        both = jnp.dot(
            jnp.concatenate([rows, rows], axis=1), ref[p], preferred_element_type=jnp.float32
        )
        one = both[0:8, :BLK]
        two = both[8:16, BLK:]
        slots_ref[pl.ds(route_ref[1, e], NF), :] = one[:NF] + one[NF:]
        slots_ref[pl.ds(route_ref[1, e + 1], NF), :] = two[:NF] + two[NF:]

    def pairs(ref, first, unroll):
        @pl.loop(0, ref.shape[0], step=unroll)
        def _(start):
            for k in range(unroll):
                pair(ref, start + k, first)

    pairs(halves_ref, 0, UNROLL)
    pairs(later_ref, halves_ref.shape[0], later_ref.shape[0])


def aloft_kernel(
    meta_ref, diffusion_ref, courant_ref, x_ref, top_ref, bottom_ref, left_ref, right_ref, out_ref, keep_ref
):
    group = pl.program_id(0) + 1

    @pl.when(group == 1)
    def _():
        keep_ref[...] = inside(meta_ref).astype(jnp.float32)

    fields = extended_group(
        meta_ref, (diffusion_ref, courant_ref), x_ref, top_ref, bottom_ref, left_ref, right_ref,
        keep_ref, group * NF,
    )
    for k, field in enumerate(fields):
        out_ref[k] = field


def finish_kernel(slots_ref, surface_ref, coef_ref, aloft_ref, state_ref, remapped_ref):
    del aloft_ref
    peers = slots_ref.shape[0] // ROWS_PER_PEER
    labels = slots_ref[pl.ds(ROWS_PER_PEER - 1, peers, stride=ROWS_PER_PEER), :].T
    row = lax.broadcasted_iota(jnp.int32, (BPD, peers), 0)
    block = jnp.where(row < CX, 2 * row, 2 * (row - CX) + 1).astype(jnp.float32)
    chosen = [(block == labels[k : k + 1]).astype(jnp.bfloat16) for k in range(CAP)]
    dims = (((1,), (0,)), ((), ()))
    for level in range(NF):
        total = jnp.zeros((BPD, BLK), jnp.float32)
        for k in range(CAP):
            data = slots_ref[pl.ds(k * NF + level, peers, stride=ROWS_PER_PEER), :]
            high = data.astype(jnp.bfloat16)
            low = (data - high.astype(jnp.float32)).astype(jnp.bfloat16)
            total += lax.dot_general(chosen[k], high, dims, preferred_element_type=jnp.float32)
            total += lax.dot_general(chosen[k], low, dims, preferred_element_type=jnp.float32)
        total = jnp.concatenate([total[:CX], total[CX:]], axis=1)
        remapped_ref[level] = total
        surface = surface_ref[level]
        state_ref[level] = surface + coef_ref[...] * jnp.tanh(total - surface)


def body(
    air_sea_state, diffusion, courant, exchange_coef, src_block, dest_peer, dest_block, remap_weight
):
    peers = lax.axis_size("gx") * lax.axis_size("gy")
    rows_out = peers * ROWS_PER_PEER
    at_x, at_y = lax.axis_index("gx"), lax.axis_index("gy")
    x = air_sea_state[0]
    smem = pl.BlockSpec(memory_space=pltpu.SMEM)
    vmem = pl.BlockSpec(memory_space=pltpu.VMEM)
    anywhere = pl.BlockSpec(memory_space=pl.ANY)

    def in_hbm(value):
        return pltpu.with_memory_space_constraint(value, pltpu.HBM)

    def limit(mib):
        return pltpu.CompilerParams(vmem_limit_bytes=mib << 20)

    meta = jnp.stack(
        [
            at_x * CX,
            at_y * CY,
            lax.axis_size("gx") * CX,
            lax.axis_size("gy") * CY,
            jnp.where(lax.axis_index("sec") == 0, STEPS_A, STEPS_O),
        ]
    ).astype(jnp.int32)
    with jax.named_scope("halo"):
        top = lax.ppermute(x[:, CX - HALO :], "gx", ring("gx", 1))
        bottom = lax.ppermute(x[:, :HALO], "gx", ring("gx", -1))

    with jax.named_scope("prepare"):
        centre = jax.ShapeDtypeStruct((CX, BLK), jnp.float32)
        halves, left, right = pl.pallas_call(
            prepare_kernel,
            in_specs=[anywhere] * 3,
            out_specs=[vmem] * 3,
            out_shape=(
                pltpu.VMEM(((N_CHUNKS - LATER) * CHUNK // 2, 2 * BLK, 2 * BLK), jnp.bfloat16),
                centre,
                centre,
            ),
            scratch_shapes=[
                pltpu.VMEM(((N_CHUNKS - LATER) * CHUNK, BLK, BLK), jnp.float32),
                pltpu.VMEM((LEV, CX, CY), jnp.float32),
                pltpu.SemaphoreType.DMA((N_CHUNKS - LATER,)),
                pltpu.SemaphoreType.DMA,
            ],
            compiler_params=limit(16),
            name="prepare",
        )(in_hbm(remap_weight[0]), in_hbm(x), meta)

    with jax.named_scope("halo"):
        side = jax.ShapeDtypeStruct((ROWS, BLK), jnp.float32)
        left, right = pl.pallas_call(
            pack_kernel, out_shape=(side, side), compiler_params=limit(2), name="pack"
        )(top, bottom, left, right)
        from_right = lax.ppermute(left, "gy", ring("gy", -1))
        from_left = lax.ppermute(right, "gy", ring("gy", 1))

    later, route, label = pl.pallas_call(
        route_kernel,
        in_specs=[anywhere, vmem, vmem, vmem, anywhere],
        out_specs=[vmem] * 3,
        out_shape=(
            pltpu.VMEM((LATER * CHUNK // 2, 2 * BLK, 2 * BLK), jnp.bfloat16),
            jax.ShapeDtypeStruct((2, EPD), jnp.int32),
            jax.ShapeDtypeStruct((peers, BLK), jnp.float32),
        ),
        scratch_shapes=[
            pltpu.VMEM((LATER * CHUNK, BLK, BLK), jnp.float32),
            pltpu.SemaphoreType.DMA((LATER,)),
        ],
        compiler_params=limit(6),
        name="route",
    )(in_hbm(remap_weight[0]), src_block, dest_peer.reshape(1, EPD), dest_block, left)

    tile = pl.BlockSpec((NF, CX, CY), lambda i: (0, 0, 0))
    edge = pl.BlockSpec((NF, HALO, CY), lambda i: (0, 0, 0))
    whole = pl.BlockSpec((ROWS, BLK), lambda i: (0, 0))
    outgoing, surface = pl.pallas_call(
        surface_kernel,
        grid=(1,),
        in_specs=[
            smem, smem, smem, smem, tile, edge, edge, whole, whole,
            pl.BlockSpec((peers, BLK), lambda i: (0, 0)), vmem, vmem,
        ],
        out_specs=[pl.BlockSpec((rows_out, BLK), lambda i: (0, 0)), tile],
        out_shape=(
            jax.ShapeDtypeStruct((rows_out, BLK), jnp.float32),
            jax.ShapeDtypeStruct((NF, CX, CY), jnp.float32),
        ),
        scratch_shapes=[
            pltpu.VMEM((BPD * 8, BLK), jnp.float32),
            pltpu.VMEM((ROWS, COLS), jnp.float32),
        ],
        compiler_params=limit(6),
        name="surface",
    )(
        meta, diffusion, courant, route, x, top, bottom, from_left, from_right, label, halves,
        later,
    )

    tile_up = pl.BlockSpec((NF, CX, CY), lambda i: (i + 1, 0, 0))
    edge_up = pl.BlockSpec((NF, HALO, CY), lambda i: (i + 1, 0, 0))
    aloft = pl.pallas_call(
        aloft_kernel,
        grid=(LEV // NF - 1,),
        in_specs=[smem, smem, smem, tile_up, edge_up, edge_up, whole, whole],
        out_specs=tile_up,
        out_shape=jax.ShapeDtypeStruct((LEV, CX, CY), jnp.float32),
        scratch_shapes=[pltpu.VMEM((ROWS, COLS), jnp.float32)],
        compiler_params=limit(4),
        name="aloft",
    )(meta, diffusion, courant, x, top, bottom, from_left, from_right)

    outgoing = lax.ppermute(outgoing, "sec", ring("sec", 1))
    incoming = lax.all_to_all(
        outgoing.reshape(peers, ROWS_PER_PEER, 1, BLK), ("gx", "gy"), split_axis=0, concat_axis=0, tiled=True
    )
    incoming = incoming.reshape(rows_out, BLK)

    new_state, remapped = pl.pallas_call(
        finish_kernel,
        grid=(1,),
        in_specs=[
            pl.BlockSpec((rows_out, BLK), lambda i: (0, 0)),
            tile,
            pl.BlockSpec((CX, CY), lambda i: (0, 0)),
            pl.BlockSpec(memory_space=pl.ANY),
        ],
        out_specs=[tile, tile],
        out_shape=(
            jax.ShapeDtypeStruct((LEV, CX, CY), jnp.float32),
            jax.ShapeDtypeStruct((NF, CX, CY), jnp.float32),
        ),
        input_output_aliases={3: 0},
        compiler_params=limit(5),
        name="finish",
    )(incoming, surface, exchange_coef[0], aloft)
    return (new_state[None], remapped[None])


def solution(mesh):
    in_specs = (
        P("sec", None, "gx", "gy"),
        P("sec", None),
        P("sec", None),
        P("sec", "gx", "gy"),
        P("sec", ("gx", "gy")),
        P("sec", ("gx", "gy"), None),
        P("sec", ("gx", "gy")),
        P("sec", ("gx", "gy"), None, None),
    )
    out_specs = (P("sec", None, "gx", "gy"), P("sec", None, "gx", "gy"))
    return jax.shard_map(body, mesh=mesh, in_specs=in_specs, out_specs=out_specs, check_vma=False)
```

```python
import jax
import jax.numpy as jnp
from jax import lax
from jax.experimental import pallas as pl
from jax.experimental.pallas import tpu as pltpu
from jax.sharding import PartitionSpec as P

LEV = 16
NF = 4
BLK = 128
CX = 48
CY = 256
BPD = 96
EPD = 192
CAP = 3
STEPS_A = 6
STEPS_O = 3
HALO = 8
ROWS = CX + 2 * HALO
COLS = CY + BLK
CHUNK = 16
N_CHUNKS = EPD // CHUNK
ROWS_PER_PEER = CAP * NF + 1
UNROLL = 28
LATER = 5
DEPTH = 4


def ring(axis, shift):
    count = lax.axis_size(axis)
    return [(i, (i + shift) % count) for i in range(count)]


def inside(meta_ref):
    row = lax.broadcasted_iota(jnp.int32, (ROWS, COLS), 0)
    col = lax.broadcasted_iota(jnp.int32, (ROWS, COLS), 1)
    row = jnp.where(row >= CX + HALO, row - ROWS, row) + meta_ref[0]
    col = jnp.where(col >= CY + BLK // 2, col - COLS, col) + meta_ref[1]
    return (row >= 0) & (row < meta_ref[2]) & (col >= 0) & (col < meta_ref[3])


def extended(tile, top, bottom, from_left, from_right, level):
    lane = lax.broadcasted_iota(jnp.int32, (ROWS, BLK), 1)
    after = pltpu.roll(from_right, (BLK - HALO * level) % BLK, 1)
    before = pltpu.roll(from_left, (2 * BLK - HALO - HALO * level) % BLK, 1)
    beyond = jnp.where(lane < HALO, after, jnp.where(lane >= BLK - HALO, before, 0.0))
    own = jnp.concatenate([tile, bottom, top], axis=0)
    return jnp.concatenate([own, beyond], axis=1)


def evolve(fields, keep_ref, rates, steps):
    def step(u, diffuse, carry_rate):
        beside = pltpu.roll(u, ROWS - 1, 0) + pltpu.roll(u, 1, 1) + pltpu.roll(u, COLS - 1, 1)
        upwind = (diffuse + carry_rate) * pltpu.roll(u, 1, 0)
        centre = (1.0 - 4.0 * diffuse - carry_rate) * u
        return (centre + upwind + diffuse * beside) * keep_ref[...]

    def advance(_, now):
        for _ in range(STEPS_O):
            now = tuple(step(u, *rate) for u, rate in zip(now, rates))
        return now

    fields = tuple(u * keep_ref[...] for u in fields)
    return lax.fori_loop(0, steps // STEPS_O, advance, fields)


def extended_group(meta_ref, rate_refs, x_ref, top_ref, bottom_ref, left_ref, right_ref, keep_ref, first):
    fields, rates = [], []
    for k in range(NF):
        fields.append(
            extended(x_ref[k], top_ref[k], bottom_ref[k], left_ref[...], right_ref[...], first + k)
        )
        rates.append(tuple(ref[0, first + k] for ref in rate_refs))
    fields = evolve(fields, keep_ref, rates, meta_ref[4])
    return [u[:CX, :CY] for u in fields]


def split_parts(w_ref, w_buf, sems, halves_ref, first):
    def fetch(part):
        rows = pl.ds(part * CHUNK, CHUNK)
        whence = w_ref.at[pl.ds((first + part) * CHUNK, CHUNK)]
        return pltpu.make_async_copy(whence, w_buf.at[rows], sems.at[part])

    def begin():
        for part in range(min(DEPTH, sems.shape[0])):
            fetch(part).start()

    def finish():
        @pl.loop(0, sems.shape[0])
        def _(part):
            fetch(part).wait()

            @pl.when(part + DEPTH < sems.shape[0])
            def _():
                fetch(part + DEPTH).start()

            for k in range(CHUNK):
                weight = w_buf[part * CHUNK + k].T
                high = weight.astype(jnp.bfloat16)
                low = (weight - high.astype(jnp.float32)).astype(jnp.bfloat16)
                pair = part * (CHUNK // 2) + k // 2
                cols = slice(k % 2 * BLK, (k % 2 + 1) * BLK)
                halves_ref[pair, :BLK, cols] = high
                halves_ref[pair, BLK:, cols] = low

    return begin, finish


def prepare_kernel(
    w_ref, x_ref, meta_ref, halves_ref, left_ref, right_ref, w_buf, x_buf, w_sems, x_sem
):
    del meta_ref
    tile = pltpu.make_async_copy(x_ref, x_buf, x_sem)
    begin, finish = split_parts(w_ref, w_buf, w_sems, halves_ref, 0)
    begin()
    tile.start()
    finish()
    tile.wait()
    lane = lax.broadcasted_iota(jnp.int32, (CX, BLK), 1) // HALO
    left = jnp.zeros((CX, BLK), jnp.float32)
    right = jnp.zeros((CX, BLK), jnp.float32)
    for level in range(LEV):
        left, right = packed(x_buf[level], left, right, lane, level)
    left_ref[...] = left
    right_ref[...] = right


def route_kernel(
    w_ref, source_ref, peer_ref, block_ref, after_ref, halves_ref, route_ref, label_ref, w_buf, sems
):
    del after_ref
    begin, finish = split_parts(w_ref, w_buf, sems, halves_ref, N_CHUNKS - sems.shape[0])
    begin()
    target = peer_ref[...]
    column = jnp.broadcast_to(target.astype(jnp.float32), (8, EPD)).T[:, :1].astype(jnp.int32)
    first = lax.broadcasted_iota(jnp.int32, (EPD, EPD), 0)
    second = lax.broadcasted_iota(jnp.int32, (EPD, EPD), 1)
    earlier = (column == target) & (first < second)
    rank = jnp.sum(earlier.astype(jnp.int32), axis=0, keepdims=True)
    route_ref[0:1] = source_ref[...] * 8
    route_ref[1:2] = target * ROWS_PER_PEER + rank * NF
    peers = label_ref.shape[0]
    to_peer = lax.broadcasted_iota(jnp.int32, (peers, EPD), 0) == target
    slot = lax.broadcasted_iota(jnp.int32, (BLK, EPD), 0) == rank
    value = jnp.where(slot, block_ref[...].astype(jnp.float32) + 1.0, 0.0)
    label_ref[...] = lax.dot_general(
        to_peer.astype(jnp.bfloat16),
        value.astype(jnp.bfloat16),
        (((1,), (1,)), ((), ())),
        preferred_element_type=jnp.float32,
    ) - 1.0
    finish()


def packed(rows, left, right, lane, level):
    left = jnp.where(lane == level, pltpu.roll(rows[:, :BLK], HALO * level, 1), left)
    shift = (HALO * level + HALO) % BLK
    right = jnp.where(lane == level, pltpu.roll(rows[:, CY - BLK :], shift, 1), right)
    return left, right


def pack_kernel(top_ref, bottom_ref, left_in, right_in, left_ref, right_ref):
    lane = lax.broadcasted_iota(jnp.int32, (2 * HALO, BLK), 1) // HALO
    left = jnp.zeros((2 * HALO, BLK), jnp.float32)
    right = jnp.zeros((2 * HALO, BLK), jnp.float32)
    for level in range(LEV):
        rows = jnp.concatenate([bottom_ref[level], top_ref[level]], axis=0)
        left, right = packed(rows, left, right, lane, level)
    left_ref[:CX] = left_in[...]
    left_ref[CX:] = left
    right_ref[:CX] = right_in[...]
    right_ref[CX:] = right


def surface_kernel(
    meta_ref, diffusion_ref, courant_ref, route_ref, x_ref, top_ref, bottom_ref, left_ref, right_ref, label_ref,
    halves_ref, later_ref, slots_ref, surface_ref, blocks, keep_ref,
):
    slots_ref[...] = jnp.zeros(slots_ref.shape, jnp.float32)
    slots_ref[pl.ds(ROWS_PER_PEER - 1, label_ref.shape[0], stride=ROWS_PER_PEER), :] = label_ref[...]
    keep_ref[...] = inside(meta_ref).astype(jnp.float32)
    fields = extended_group(
        meta_ref, (diffusion_ref, courant_ref), x_ref, top_ref, bottom_ref, left_ref, right_ref,
        keep_ref, 0,
    )
    for level, field in enumerate(fields):
        surface_ref[level] = field
        high = field.astype(jnp.bfloat16).astype(jnp.float32)
        low = field - high
        for half in range(2):
            cols = slice(half * BLK, (half + 1) * BLK)
            blocks[pl.ds(half * 8 + level, CX, stride=16), :] = high[:, cols]
            blocks[pl.ds(half * 8 + NF + level, CX, stride=16), :] = low[:, cols]

    def pair(ref, p, first):
        def picked(e):
            return blocks[pl.ds(pl.multiple_of(route_ref[0, e], 8), 8), :]

        e = 2 * (p + first)
        rows = jnp.concatenate([picked(e), picked(e + 1)], axis=0).astype(jnp.bfloat16)
        both = jnp.dot(
            jnp.concatenate([rows, rows], axis=1), ref[p], preferred_element_type=jnp.float32
        )
        one = both[0:8, :BLK]
        two = both[8:16, BLK:]
        slots_ref[pl.ds(route_ref[1, e], NF), :] = one[:NF] + one[NF:]
        slots_ref[pl.ds(route_ref[1, e + 1], NF), :] = two[:NF] + two[NF:]

    def pairs(ref, first, unroll):
        @pl.loop(0, ref.shape[0], step=unroll)
        def _(start):
            for k in range(unroll):
                pair(ref, start + k, first)

    pairs(halves_ref, 0, UNROLL)
    pairs(later_ref, halves_ref.shape[0], later_ref.shape[0])


def aloft_kernel(
    meta_ref, diffusion_ref, courant_ref, x_ref, top_ref, bottom_ref, left_ref, right_ref, out_ref, keep_ref
):
    group = pl.program_id(0) + 1

    @pl.when(group == 1)
    def _():
        keep_ref[...] = inside(meta_ref).astype(jnp.float32)

    fields = extended_group(
        meta_ref, (diffusion_ref, courant_ref), x_ref, top_ref, bottom_ref, left_ref, right_ref,
        keep_ref, group * NF,
    )
    for k, field in enumerate(fields):
        out_ref[k] = field


def combine_kernel(slots_ref, total_ref):
    peers = slots_ref.shape[0] // ROWS_PER_PEER
    labels = slots_ref[pl.ds(ROWS_PER_PEER - 1, peers, stride=ROWS_PER_PEER), :].T
    row = lax.broadcasted_iota(jnp.int32, (BPD, peers), 0)
    block = jnp.where(row < CX, 2 * row, 2 * (row - CX) + 1).astype(jnp.float32)
    chosen = [(block == labels[k : k + 1]).astype(jnp.bfloat16) for k in range(CAP)]
    dims = (((1,), (0,)), ((), ()))
    for level in range(NF):
        total = jnp.zeros((BPD, BLK), jnp.float32)
        for k in range(CAP):
            data = slots_ref[pl.ds(k * NF + level, peers, stride=ROWS_PER_PEER), :]
            high = data.astype(jnp.bfloat16)
            low = (data - high.astype(jnp.float32)).astype(jnp.bfloat16)
            total += lax.dot_general(chosen[k], high, dims, preferred_element_type=jnp.float32)
            total += lax.dot_general(chosen[k], low, dims, preferred_element_type=jnp.float32)
        total_ref[level] = jnp.concatenate([total[:CX], total[CX:]], axis=1)


def finish_kernel(total_ref, surface_ref, coef_ref, aloft_ref, state_ref, remapped_ref):
    del aloft_ref
    for level in range(NF):
        total = total_ref[level]
        remapped_ref[level] = total
        surface = surface_ref[level]
        state_ref[level] = surface + coef_ref[...] * jnp.tanh(total - surface)


def body(
    air_sea_state, diffusion, courant, exchange_coef, src_block, dest_peer, dest_block, remap_weight
):
    peers = lax.axis_size("gx") * lax.axis_size("gy")
    rows_out = peers * ROWS_PER_PEER
    at_x, at_y = lax.axis_index("gx"), lax.axis_index("gy")
    x = air_sea_state[0]
    smem = pl.BlockSpec(memory_space=pltpu.SMEM)
    vmem = pl.BlockSpec(memory_space=pltpu.VMEM)
    anywhere = pl.BlockSpec(memory_space=pl.ANY)

    def in_hbm(value):
        return pltpu.with_memory_space_constraint(value, pltpu.HBM)

    def limit(mib):
        return pltpu.CompilerParams(vmem_limit_bytes=mib << 20)

    meta = jnp.stack(
        [
            at_x * CX,
            at_y * CY,
            lax.axis_size("gx") * CX,
            lax.axis_size("gy") * CY,
            jnp.where(lax.axis_index("sec") == 0, STEPS_A, STEPS_O),
        ]
    ).astype(jnp.int32)
    with jax.named_scope("halo"):
        top = lax.ppermute(x[:, CX - HALO :], "gx", ring("gx", 1))
        bottom = lax.ppermute(x[:, :HALO], "gx", ring("gx", -1))

    with jax.named_scope("prepare"):
        centre = jax.ShapeDtypeStruct((CX, BLK), jnp.float32)
        halves, left, right = pl.pallas_call(
            prepare_kernel,
            in_specs=[anywhere] * 3,
            out_specs=[vmem] * 3,
            out_shape=(
                pltpu.VMEM(((N_CHUNKS - LATER) * CHUNK // 2, 2 * BLK, 2 * BLK), jnp.bfloat16),
                centre,
                centre,
            ),
            scratch_shapes=[
                pltpu.VMEM(((N_CHUNKS - LATER) * CHUNK, BLK, BLK), jnp.float32),
                pltpu.VMEM((LEV, CX, CY), jnp.float32),
                pltpu.SemaphoreType.DMA((N_CHUNKS - LATER,)),
                pltpu.SemaphoreType.DMA,
            ],
            compiler_params=limit(16),
            name="prepare",
        )(in_hbm(remap_weight[0]), in_hbm(x), meta)

    with jax.named_scope("halo"):
        side = jax.ShapeDtypeStruct((ROWS, BLK), jnp.float32)
        left, right = pl.pallas_call(
            pack_kernel, out_shape=(side, side), compiler_params=limit(2), name="pack"
        )(top, bottom, left, right)
        from_right = lax.ppermute(left, "gy", ring("gy", -1))
        from_left = lax.ppermute(right, "gy", ring("gy", 1))

    later, route, label = pl.pallas_call(
        route_kernel,
        in_specs=[anywhere, vmem, vmem, vmem, anywhere],
        out_specs=[vmem] * 3,
        out_shape=(
            pltpu.VMEM((LATER * CHUNK // 2, 2 * BLK, 2 * BLK), jnp.bfloat16),
            jax.ShapeDtypeStruct((2, EPD), jnp.int32),
            jax.ShapeDtypeStruct((peers, BLK), jnp.float32),
        ),
        scratch_shapes=[
            pltpu.VMEM((LATER * CHUNK, BLK, BLK), jnp.float32),
            pltpu.SemaphoreType.DMA((LATER,)),
        ],
        compiler_params=limit(6),
        name="route",
    )(in_hbm(remap_weight[0]), src_block, dest_peer.reshape(1, EPD), dest_block, left)

    tile = pl.BlockSpec((NF, CX, CY), lambda i: (0, 0, 0))
    edge = pl.BlockSpec((NF, HALO, CY), lambda i: (0, 0, 0))
    whole = pl.BlockSpec((ROWS, BLK), lambda i: (0, 0))
    outgoing, surface = pl.pallas_call(
        surface_kernel,
        grid=(1,),
        in_specs=[
            smem, smem, smem, smem, tile, edge, edge, whole, whole,
            pl.BlockSpec((peers, BLK), lambda i: (0, 0)), vmem, vmem,
        ],
        out_specs=[pl.BlockSpec((rows_out, BLK), lambda i: (0, 0)), tile],
        out_shape=(
            jax.ShapeDtypeStruct((rows_out, BLK), jnp.float32),
            jax.ShapeDtypeStruct((NF, CX, CY), jnp.float32),
        ),
        scratch_shapes=[
            pltpu.VMEM((BPD * 8, BLK), jnp.float32),
            pltpu.VMEM((ROWS, COLS), jnp.float32),
        ],
        compiler_params=limit(6),
        name="surface",
    )(
        meta, diffusion, courant, route, x, top, bottom, from_left, from_right, label, halves,
        later,
    )

    tile_up = pl.BlockSpec((NF, CX, CY), lambda i: (i + 1, 0, 0))
    edge_up = pl.BlockSpec((NF, HALO, CY), lambda i: (i + 1, 0, 0))
    aloft = pl.pallas_call(
        aloft_kernel,
        grid=(LEV // NF - 1,),
        in_specs=[smem, smem, smem, tile_up, edge_up, edge_up, whole, whole],
        out_specs=tile_up,
        out_shape=jax.ShapeDtypeStruct((LEV, CX, CY), jnp.float32),
        scratch_shapes=[pltpu.VMEM((ROWS, COLS), jnp.float32)],
        compiler_params=limit(4),
        name="aloft",
    )(meta, diffusion, courant, x, top, bottom, from_left, from_right)

    incoming = lax.all_to_all(
        outgoing.reshape(peers, ROWS_PER_PEER, 1, BLK), ("gx", "gy"), split_axis=0, concat_axis=0, tiled=True
    )
    incoming = incoming.reshape(rows_out, BLK)
    incoming, aloft = lax.optimization_barrier((incoming, aloft))
    total = pl.pallas_call(
        combine_kernel,
        out_shape=jax.ShapeDtypeStruct((NF, CX, CY), jnp.float32),
        compiler_params=limit(3),
        name="combine",
    )(incoming)
    total = lax.ppermute(total, "sec", ring("sec", 1))

    new_state, remapped = pl.pallas_call(
        finish_kernel,
        grid=(1,),
        in_specs=[
            tile,
            tile,
            pl.BlockSpec((CX, CY), lambda i: (0, 0)),
            pl.BlockSpec(memory_space=pl.ANY),
        ],
        out_specs=[tile, tile],
        out_shape=(
            jax.ShapeDtypeStruct((LEV, CX, CY), jnp.float32),
            jax.ShapeDtypeStruct((NF, CX, CY), jnp.float32),
        ),
        input_output_aliases={3: 0},
        compiler_params=limit(5),
        name="finish",
    )(total, surface, exchange_coef[0], aloft)
    return (new_state[None], remapped[None])


def solution(mesh):
    in_specs = (
        P("sec", None, "gx", "gy"),
        P("sec", None),
        P("sec", None),
        P("sec", "gx", "gy"),
        P("sec", ("gx", "gy")),
        P("sec", ("gx", "gy"), None),
        P("sec", ("gx", "gy")),
        P("sec", ("gx", "gy"), None, None),
    )
    out_specs = (P("sec", None, "gx", "gy"), P("sec", None, "gx", "gy"))
    return jax.shard_map(body, mesh=mesh, in_specs=in_specs, out_specs=out_specs, check_vma=False)
```

```python
import jax
import jax.numpy as jnp
from jax import lax
from jax.experimental import pallas as pl
from jax.experimental.pallas import tpu as pltpu
from jax.sharding import PartitionSpec as P

LEV = 16
NF = 4
BLK = 128
CX = 48
CY = 256
BPD = 96
EPD = 192
CAP = 3
STEPS_A = 6
STEPS_O = 3
HALO = 8
ROWS = CX + 2 * HALO
COLS = CY + BLK
CHUNK = 16
N_CHUNKS = EPD // CHUNK
ROWS_PER_PEER = CAP * NF + 1
UNROLL = 24
LATER = 6
DEPTH = 5


def ring(axis, shift):
    count = lax.axis_size(axis)
    return [(i, (i + shift) % count) for i in range(count)]


def inside(meta_ref):
    row = lax.broadcasted_iota(jnp.int32, (ROWS, COLS), 0)
    col = lax.broadcasted_iota(jnp.int32, (ROWS, COLS), 1)
    row = jnp.where(row >= CX + HALO, row - ROWS, row) + meta_ref[0]
    col = jnp.where(col >= CY + BLK // 2, col - COLS, col) + meta_ref[1]
    return (row >= 0) & (row < meta_ref[2]) & (col >= 0) & (col < meta_ref[3])


def extended(tile, top, bottom, from_left, from_right, level):
    lane = lax.broadcasted_iota(jnp.int32, (ROWS, BLK), 1)
    after = pltpu.roll(from_right, (BLK - HALO * level) % BLK, 1)
    before = pltpu.roll(from_left, (2 * BLK - HALO - HALO * level) % BLK, 1)
    beyond = jnp.where(lane < HALO, after, jnp.where(lane >= BLK - HALO, before, 0.0))
    own = jnp.concatenate([tile, bottom, top], axis=0)
    return jnp.concatenate([own, beyond], axis=1)


def evolve(fields, keep_ref, rates, steps):
    def step(u, diffuse, carry_rate):
        beside = pltpu.roll(u, ROWS - 1, 0) + pltpu.roll(u, 1, 1) + pltpu.roll(u, COLS - 1, 1)
        upwind = (diffuse + carry_rate) * pltpu.roll(u, 1, 0)
        centre = (1.0 - 4.0 * diffuse - carry_rate) * u
        return (centre + upwind + diffuse * beside) * keep_ref[...]

    def advance(_, now):
        for _ in range(STEPS_O):
            now = tuple(step(u, *rate) for u, rate in zip(now, rates))
        return now

    fields = tuple(u * keep_ref[...] for u in fields)
    return lax.fori_loop(0, steps // STEPS_O, advance, fields)


def extended_group(meta_ref, rate_refs, x_ref, top_ref, bottom_ref, left_ref, right_ref, keep_ref, first):
    fields, rates = [], []
    for k in range(NF):
        fields.append(
            extended(x_ref[k], top_ref[k], bottom_ref[k], left_ref[...], right_ref[...], first + k)
        )
        rates.append(tuple(ref[0, first + k] for ref in rate_refs))
    fields = evolve(fields, keep_ref, rates, meta_ref[4])
    return [u[:CX, :CY] for u in fields]


def split_parts(w_ref, w_buf, sems, halves_ref, first):
    def fetch(part):
        rows = pl.ds(part * CHUNK, CHUNK)
        whence = w_ref.at[pl.ds((first + part) * CHUNK, CHUNK)]
        return pltpu.make_async_copy(whence, w_buf.at[rows], sems.at[part])

    def begin():
        for part in range(min(DEPTH, sems.shape[0])):
            fetch(part).start()

    def finish():
        @pl.loop(0, sems.shape[0])
        def _(part):
            fetch(part).wait()

            @pl.when(part + DEPTH < sems.shape[0])
            def _():
                fetch(part + DEPTH).start()

            for k in range(CHUNK):
                weight = w_buf[part * CHUNK + k].T
                high = weight.astype(jnp.bfloat16)
                low = (weight - high.astype(jnp.float32)).astype(jnp.bfloat16)
                pair = part * (CHUNK // 2) + k // 2
                cols = slice(k % 2 * BLK, (k % 2 + 1) * BLK)
                halves_ref[pair, :BLK, cols] = high
                halves_ref[pair, BLK:, cols] = low

    return begin, finish


def prepare_kernel(
    w_ref, x_ref, meta_ref, halves_ref, left_ref, right_ref, w_buf, x_buf, w_sems, x_sem
):
    del meta_ref
    tile = pltpu.make_async_copy(x_ref, x_buf, x_sem)
    begin, finish = split_parts(w_ref, w_buf, w_sems, halves_ref, 0)
    begin()
    tile.start()
    finish()
    tile.wait()
    lane = lax.broadcasted_iota(jnp.int32, (CX, BLK), 1) // HALO
    left = jnp.zeros((CX, BLK), jnp.float32)
    right = jnp.zeros((CX, BLK), jnp.float32)
    for level in range(LEV):
        left, right = packed(x_buf[level], left, right, lane, level)
    left_ref[...] = left
    right_ref[...] = right


def route_kernel(
    w_ref, source_ref, peer_ref, block_ref, after_ref, halves_ref, route_ref, label_ref, w_buf, sems
):
    del after_ref
    begin, finish = split_parts(w_ref, w_buf, sems, halves_ref, N_CHUNKS - sems.shape[0])
    begin()
    target = peer_ref[...]
    column = jnp.broadcast_to(target.astype(jnp.float32), (8, EPD)).T[:, :1].astype(jnp.int32)
    first = lax.broadcasted_iota(jnp.int32, (EPD, EPD), 0)
    second = lax.broadcasted_iota(jnp.int32, (EPD, EPD), 1)
    earlier = (column == target) & (first < second)
    rank = jnp.sum(earlier.astype(jnp.int32), axis=0, keepdims=True)
    route_ref[0:1] = source_ref[...] * 8
    route_ref[1:2] = target * ROWS_PER_PEER + rank * NF
    peers = label_ref.shape[0]
    to_peer = lax.broadcasted_iota(jnp.int32, (peers, EPD), 0) == target
    slot = lax.broadcasted_iota(jnp.int32, (BLK, EPD), 0) == rank
    value = jnp.where(slot, block_ref[...].astype(jnp.float32) + 1.0, 0.0)
    label_ref[...] = lax.dot_general(
        to_peer.astype(jnp.bfloat16),
        value.astype(jnp.bfloat16),
        (((1,), (1,)), ((), ())),
        preferred_element_type=jnp.float32,
    ) - 1.0
    finish()


def packed(rows, left, right, lane, level):
    left = jnp.where(lane == level, pltpu.roll(rows[:, :BLK], HALO * level, 1), left)
    shift = (HALO * level + HALO) % BLK
    right = jnp.where(lane == level, pltpu.roll(rows[:, CY - BLK :], shift, 1), right)
    return left, right


def pack_kernel(top_ref, bottom_ref, left_in, right_in, left_ref, right_ref):
    lane = lax.broadcasted_iota(jnp.int32, (2 * HALO, BLK), 1) // HALO
    left = jnp.zeros((2 * HALO, BLK), jnp.float32)
    right = jnp.zeros((2 * HALO, BLK), jnp.float32)
    for level in range(LEV):
        rows = jnp.concatenate([bottom_ref[level], top_ref[level]], axis=0)
        left, right = packed(rows, left, right, lane, level)
    left_ref[:CX] = left_in[...]
    left_ref[CX:] = left
    right_ref[:CX] = right_in[...]
    right_ref[CX:] = right


def surface_kernel(
    meta_ref, diffusion_ref, courant_ref, route_ref, x_ref, top_ref, bottom_ref, left_ref, right_ref, label_ref,
    halves_ref, later_ref, slots_ref, surface_ref, blocks, keep_ref,
):
    slots_ref[...] = jnp.zeros(slots_ref.shape, jnp.float32)
    slots_ref[pl.ds(ROWS_PER_PEER - 1, label_ref.shape[0], stride=ROWS_PER_PEER), :] = label_ref[...]
    keep_ref[...] = inside(meta_ref).astype(jnp.float32)
    fields = extended_group(
        meta_ref, (diffusion_ref, courant_ref), x_ref, top_ref, bottom_ref, left_ref, right_ref,
        keep_ref, 0,
    )
    for level, field in enumerate(fields):
        surface_ref[level] = field
        high = field.astype(jnp.bfloat16).astype(jnp.float32)
        low = field - high
        for half in range(2):
            cols = slice(half * BLK, (half + 1) * BLK)
            blocks[pl.ds(half * 8 + level, CX, stride=16), :] = high[:, cols]
            blocks[pl.ds(half * 8 + NF + level, CX, stride=16), :] = low[:, cols]

    def pair(ref, p, first):
        def picked(e):
            return blocks[pl.ds(pl.multiple_of(route_ref[0, e], 8), 8), :]

        e = 2 * (p + first)
        rows = jnp.concatenate([picked(e), picked(e + 1)], axis=0).astype(jnp.bfloat16)
        both = jnp.dot(
            jnp.concatenate([rows, rows], axis=1), ref[p], preferred_element_type=jnp.float32
        )
        one = both[0:8, :BLK]
        two = both[8:16, BLK:]
        slots_ref[pl.ds(route_ref[1, e], NF), :] = one[:NF] + one[NF:]
        slots_ref[pl.ds(route_ref[1, e + 1], NF), :] = two[:NF] + two[NF:]

    def pairs(ref, first, unroll):
        @pl.loop(0, ref.shape[0], step=unroll)
        def _(start):
            for k in range(unroll):
                pair(ref, start + k, first)

    pairs(halves_ref, 0, UNROLL)
    pairs(later_ref, halves_ref.shape[0], later_ref.shape[0])


def aloft_kernel(
    meta_ref, diffusion_ref, courant_ref, x_ref, top_ref, bottom_ref, left_ref, right_ref, out_ref, keep_ref
):
    group = pl.program_id(0) + 1

    @pl.when(group == 1)
    def _():
        keep_ref[...] = inside(meta_ref).astype(jnp.float32)

    fields = extended_group(
        meta_ref, (diffusion_ref, courant_ref), x_ref, top_ref, bottom_ref, left_ref, right_ref,
        keep_ref, group * NF,
    )
    for k, field in enumerate(fields):
        out_ref[k] = field


def combine_kernel(slots_ref, total_ref):
    peers = slots_ref.shape[0] // ROWS_PER_PEER
    labels = slots_ref[pl.ds(ROWS_PER_PEER - 1, peers, stride=ROWS_PER_PEER), :].T
    row = lax.broadcasted_iota(jnp.int32, (BPD, peers), 0)
    block = jnp.where(row < CX, 2 * row, 2 * (row - CX) + 1).astype(jnp.float32)
    chosen = [(block == labels[k : k + 1]).astype(jnp.bfloat16) for k in range(CAP)]
    dims = (((1,), (0,)), ((), ()))
    for level in range(NF):
        total = jnp.zeros((BPD, BLK), jnp.float32)
        for k in range(CAP):
            data = slots_ref[pl.ds(k * NF + level, peers, stride=ROWS_PER_PEER), :]
            high = data.astype(jnp.bfloat16)
            low = (data - high.astype(jnp.float32)).astype(jnp.bfloat16)
            total += lax.dot_general(chosen[k], high, dims, preferred_element_type=jnp.float32)
            total += lax.dot_general(chosen[k], low, dims, preferred_element_type=jnp.float32)
        total_ref[level] = jnp.concatenate([total[:CX], total[CX:]], axis=1)


def finish_kernel(total_ref, surface_ref, coef_ref, aloft_ref, state_ref, remapped_ref):
    del aloft_ref
    for level in range(NF):
        total = total_ref[level]
        remapped_ref[level] = total
        surface = surface_ref[level]
        state_ref[level] = surface + coef_ref[...] * jnp.tanh(total - surface)


def body(
    air_sea_state, diffusion, courant, exchange_coef, src_block, dest_peer, dest_block, remap_weight
):
    peers = lax.axis_size("gx") * lax.axis_size("gy")
    rows_out = peers * ROWS_PER_PEER
    at_x, at_y = lax.axis_index("gx"), lax.axis_index("gy")
    x = air_sea_state[0]
    smem = pl.BlockSpec(memory_space=pltpu.SMEM)
    vmem = pl.BlockSpec(memory_space=pltpu.VMEM)
    anywhere = pl.BlockSpec(memory_space=pl.ANY)

    def in_hbm(value):
        return pltpu.with_memory_space_constraint(value, pltpu.HBM)

    def limit(mib):
        return pltpu.CompilerParams(vmem_limit_bytes=mib << 20)

    meta = jnp.stack(
        [
            at_x * CX,
            at_y * CY,
            lax.axis_size("gx") * CX,
            lax.axis_size("gy") * CY,
            jnp.where(lax.axis_index("sec") == 0, STEPS_A, STEPS_O),
        ]
    ).astype(jnp.int32)
    with jax.named_scope("halo"):
        top = lax.ppermute(x[:, CX - HALO :], "gx", ring("gx", 1))
        bottom = lax.ppermute(x[:, :HALO], "gx", ring("gx", -1))

    with jax.named_scope("prepare"):
        centre = jax.ShapeDtypeStruct((CX, BLK), jnp.float32)
        halves, left, right = pl.pallas_call(
            prepare_kernel,
            in_specs=[anywhere] * 3,
            out_specs=[vmem] * 3,
            out_shape=(
                pltpu.VMEM(((N_CHUNKS - LATER) * CHUNK // 2, 2 * BLK, 2 * BLK), jnp.bfloat16),
                centre,
                centre,
            ),
            scratch_shapes=[
                pltpu.VMEM(((N_CHUNKS - LATER) * CHUNK, BLK, BLK), jnp.float32),
                pltpu.VMEM((LEV, CX, CY), jnp.float32),
                pltpu.SemaphoreType.DMA((N_CHUNKS - LATER,)),
                pltpu.SemaphoreType.DMA,
            ],
            compiler_params=limit(16),
            name="prepare",
        )(in_hbm(remap_weight[0]), in_hbm(x), meta)

    with jax.named_scope("halo"):
        side = jax.ShapeDtypeStruct((ROWS, BLK), jnp.float32)
        left, right = pl.pallas_call(
            pack_kernel, out_shape=(side, side), compiler_params=limit(2), name="pack"
        )(top, bottom, left, right)
        from_right = lax.ppermute(left, "gy", ring("gy", -1))
        from_left = lax.ppermute(right, "gy", ring("gy", 1))

    later, route, label = pl.pallas_call(
        route_kernel,
        in_specs=[anywhere, vmem, vmem, vmem, anywhere],
        out_specs=[vmem] * 3,
        out_shape=(
            pltpu.VMEM((LATER * CHUNK // 2, 2 * BLK, 2 * BLK), jnp.bfloat16),
            jax.ShapeDtypeStruct((2, EPD), jnp.int32),
            jax.ShapeDtypeStruct((peers, BLK), jnp.float32),
        ),
        scratch_shapes=[
            pltpu.VMEM((LATER * CHUNK, BLK, BLK), jnp.float32),
            pltpu.SemaphoreType.DMA((LATER,)),
        ],
        compiler_params=limit(10),
        name="route",
    )(in_hbm(remap_weight[0]), src_block, dest_peer.reshape(1, EPD), dest_block, left)

    tile = pl.BlockSpec((NF, CX, CY), lambda i: (0, 0, 0))
    edge = pl.BlockSpec((NF, HALO, CY), lambda i: (0, 0, 0))
    whole = pl.BlockSpec((ROWS, BLK), lambda i: (0, 0))
    outgoing, surface = pl.pallas_call(
        surface_kernel,
        grid=(1,),
        in_specs=[
            smem, smem, smem, smem, tile, edge, edge, whole, whole,
            pl.BlockSpec((peers, BLK), lambda i: (0, 0)), vmem, vmem,
        ],
        out_specs=[pl.BlockSpec((rows_out, BLK), lambda i: (0, 0)), tile],
        out_shape=(
            jax.ShapeDtypeStruct((rows_out, BLK), jnp.float32),
            jax.ShapeDtypeStruct((NF, CX, CY), jnp.float32),
        ),
        scratch_shapes=[
            pltpu.VMEM((BPD * 8, BLK), jnp.float32),
            pltpu.VMEM((ROWS, COLS), jnp.float32),
        ],
        compiler_params=limit(6),
        name="surface",
    )(
        meta, diffusion, courant, route, x, top, bottom, from_left, from_right, label, halves,
        later,
    )

    tile_up = pl.BlockSpec((NF, CX, CY), lambda i: (i + 1, 0, 0))
    edge_up = pl.BlockSpec((NF, HALO, CY), lambda i: (i + 1, 0, 0))
    aloft = pl.pallas_call(
        aloft_kernel,
        grid=(LEV // NF - 1,),
        in_specs=[smem, smem, smem, tile_up, edge_up, edge_up, whole, whole],
        out_specs=tile_up,
        out_shape=jax.ShapeDtypeStruct((LEV, CX, CY), jnp.float32),
        scratch_shapes=[pltpu.VMEM((ROWS, COLS), jnp.float32)],
        compiler_params=limit(4),
        name="aloft",
    )(meta, diffusion, courant, x, top, bottom, from_left, from_right)

    incoming = lax.all_to_all(
        outgoing.reshape(peers, ROWS_PER_PEER, 1, BLK), ("gx", "gy"), split_axis=0, concat_axis=0, tiled=True
    )
    incoming = incoming.reshape(rows_out, BLK)
    incoming, aloft = lax.optimization_barrier((incoming, aloft))
    total = pl.pallas_call(
        combine_kernel,
        out_shape=jax.ShapeDtypeStruct((NF, CX, CY), jnp.float32),
        compiler_params=limit(3),
        name="combine",
    )(incoming)
    total = lax.ppermute(total, "sec", ring("sec", 1))

    new_state, remapped = pl.pallas_call(
        finish_kernel,
        grid=(1,),
        in_specs=[
            tile,
            tile,
            pl.BlockSpec((CX, CY), lambda i: (0, 0)),
            pl.BlockSpec(memory_space=pl.ANY),
        ],
        out_specs=[tile, tile],
        out_shape=(
            jax.ShapeDtypeStruct((LEV, CX, CY), jnp.float32),
            jax.ShapeDtypeStruct((NF, CX, CY), jnp.float32),
        ),
        input_output_aliases={3: 0},
        compiler_params=limit(5),
        name="finish",
    )(total, surface, exchange_coef[0], aloft)
    return (new_state[None], remapped[None])


def solution(mesh):
    in_specs = (
        P("sec", None, "gx", "gy"),
        P("sec", None),
        P("sec", None),
        P("sec", "gx", "gy"),
        P("sec", ("gx", "gy")),
        P("sec", ("gx", "gy"), None),
        P("sec", ("gx", "gy")),
        P("sec", ("gx", "gy"), None, None),
    )
    out_specs = (P("sec", None, "gx", "gy"), P("sec", None, "gx", "gy"))
    return jax.shard_map(body, mesh=mesh, in_specs=in_specs, out_specs=out_specs, check_vma=False)
```
